256 devices in a mesh: cache: 64 (over y, z, core), group: 4 (over x).
Axes of the slice: x: 4, y: 4, z: 8, core: 2. Of those that a mesh axis runs over, the one named last changes fastest.
Arguments:
- queries: bfloat16 [256, 4096], P('cache'), may hold values from -240 to 240
- request_of: int32 [256], P('cache'), may hold values from 0 to 15, as said below
- selected: int32 [256, 8, 4], P('cache', 'group'), may hold values from 0 to 127, as said below
- cache_keys: bfloat16 [16, 8, 16384, 128], P(None, 'group', 'cache'), may hold values from -6 to 6
- cache_values: bfloat16 [16, 8, 16384, 128], P(None, 'group', 'cache'), may hold values from -6 to 6
- recent_keys: bfloat16 [256, 8, 1024, 128], P('cache', None, 'group'), may hold values from -6 to 6
- recent_values: bfloat16 [256, 8, 1024, 128], P('cache', None, 'group'), may hold values from -6 to 6
Outputs:
- attended: bfloat16 [256, 4096], P('cache', 'group')
The draws below stay inside these ranges and needn't reach their ends.
Inputs may be any that keep to these rules, and one draw needn't show every extreme that they name: `request_of`: each prompt is read by exactly 16 slots. `selected`: for each slot and key-value head the 4 block ids have distinct owners id // 2; the 4 slots of one index of cache, with the key-value heads of one index of group, select at most 1 block held by any one owner, and exactly 1 from some owner.
All inputs are finite; a program needn't handle non-finite values.
Results may differ from the reference program's by a relative error of at most 0.0015.
Values may be sent and summed in bfloat16 or wider, within the bound.
A program may use at most 64 MiB of HBM per device.

```python
import jax
import jax.numpy as jnp
from jax import lax

QH = 32
KVH = 8
HD = 128
BLOCK = 128
TOPK = 4
RECENT = 1024
REQ_GRP = 4
BLK_DEV = 2
REQS = 256
PROMPTS = 16
NBLK = 128
N_CACHE = 64
N_GROUP = 4


def draw_queries(key, part):
    base_key = jax.random.fold_in(jax.random.fold_in(key, 7), 0)
    base = jnp.clip(jax.random.normal(base_key, (REQS, QH, HD), jnp.float32), -6.0, 6.0)
    return base.reshape(REQS, QH * HD).astype(jnp.bfloat16)


def draw_request_of(key, part):
    order = jax.random.permutation(jax.random.fold_in(key, 13), REQS)
    return (order.astype(jnp.int32) % PROMPTS).astype(jnp.int32)


def draw_selected(key, part):
    mine_heads = KVH // N_GROUP
    wanted = REQ_GRP * mine_heads * TOPK
    order_key, local_key = jax.random.split(jax.random.fold_in(key, 11))
    scores = jax.random.randint(order_key, (N_CACHE, N_GROUP, N_CACHE), 0, 65536).astype(jnp.int32)
    scores = scores * N_CACHE + jnp.arange(N_CACHE, dtype=jnp.int32)
    owner_order = jnp.argsort(scores, axis=-1, stable=True).astype(jnp.int32)
    position = jnp.arange(wanted, dtype=jnp.int32) % N_CACHE
    owners = owner_order[:, :, position]
    owners = owners.reshape(N_CACHE, N_GROUP, REQ_GRP, mine_heads, TOPK)
    owners = jnp.transpose(owners, (0, 2, 1, 3, 4)).reshape(REQS, KVH, TOPK)
    local_block = jax.random.randint(local_key, (REQS, KVH, TOPK), 0, BLK_DEV).astype(jnp.int32)
    return (owners * BLK_DEV + local_block).astype(jnp.int32)


def block_levels(own_key, dims, shards, least, largest):
    level, own = 1.0, jax.random.fold_in(own_key, 6)
    for axis_at, parts in shards:
        heights = jnp.exp(jax.random.uniform(jax.random.fold_in(own, axis_at), (parts,), jnp.float32, least / len(shards), largest / len(shards)))
        level = level * jnp.repeat(heights, dims[axis_at] // parts).reshape([-1 if axis == axis_at else 1 for axis in range(len(dims))])
    return level


def normal_values(key, extent, scale, most, shards=(), kind=jnp.bfloat16):
    gain = block_levels(key, extent, shards, -0.22, 0.18) if shards else 1.0
    values = jax.random.normal(key, extent, jnp.float32) * scale * gain
    return jnp.minimum(jnp.maximum(values, -most), most).astype(kind)


def setup_inputs(seed: int = 0) -> dict:
    keys = jax.random.split(jax.random.key(seed), 8)
    return {
        "queries": draw_queries(jax.random.fold_in(keys[7], 71), 0),
        "request_of": draw_request_of(jax.random.fold_in(keys[7], 71), 0),
        "selected": draw_selected(jax.random.fold_in(keys[7], 71), 0),
        "cache_keys": normal_values(keys[3], (PROMPTS, KVH, NBLK * BLOCK, HD), 1.0, 6.0, ((1, 4), (2, 64))),
        "cache_values": normal_values(keys[4], (PROMPTS, KVH, NBLK * BLOCK, HD), 1.0, 6.0, ((1, 4), (2, 64))),
        "recent_keys": normal_values(keys[5], (REQS, KVH, RECENT, HD), 1.0, 6.0, ((0, 64), (2, 4))),
        "recent_values": normal_values(keys[6], (REQS, KVH, RECENT, HD), 1.0, 6.0, ((0, 64), (2, 4))),
    }


def reference(queries, request_of, selected, cache_keys, cache_values, recent_keys, recent_values):
    per_kv = QH // KVH
    score_scale = HD ** -0.5
    head_index = jnp.arange(KVH, dtype=jnp.int32)[:, None]

    def per_slot(slot):
        request = request_of[slot]
        selection = selected[slot]
        key_blocks = cache_keys[request].reshape(KVH, NBLK, BLOCK, HD)
        value_blocks = cache_values[request].reshape(KVH, NBLK, BLOCK, HD)
        picked_keys = key_blocks[head_index, selection].reshape(KVH, TOPK * BLOCK, HD)
        picked_values = value_blocks[head_index, selection].reshape(KVH, TOPK * BLOCK, HD)
        key_rows = jnp.concatenate([picked_keys, recent_keys[slot]], axis=1).astype(jnp.float32)
        value_rows = jnp.concatenate([picked_values, recent_values[slot]], axis=1).astype(jnp.float32)
        query_heads = queries[slot].reshape(KVH, per_kv, HD).astype(jnp.float32)
        scores = jnp.einsum("hgd,hnd->hgn", query_heads, key_rows, precision=lax.Precision.HIGHEST) * score_scale
        weights = jax.nn.softmax(scores, axis=-1)
        result = jnp.einsum("hgn,hnd->hgd", weights, value_rows, precision=lax.Precision.HIGHEST)
        return result.reshape(QH * HD).astype(jnp.bfloat16)

    return lax.map(per_slot, jnp.arange(REQS, dtype=jnp.int32))
```

```python
import functools

import jax
import jax.numpy as jnp
from jax import lax
from jax.experimental import pallas as pl
from jax.experimental.pallas import tpu as pltpu
from jax.sharding import PartitionSpec as P

MESH = pl.DeviceIdType.MESH
NY, NZ, NC, NG = 4, 8, 2, 4
PEERS = NY * NZ * NC
ROWS, HEADS, PER_KV, TOP = 4, 2, 4, 4
KVH, HD, BLOCK = 8, 128, 128
RECENT = 256
SCALE = HD ** (-0.5)
MSG = 6
RES = 5
WANTED = ROWS * HEADS * TOP


def signed(j):
    return ((j + 1) // 2) * (2 * (j % 2) - 1)


def split_position(cache):
    return cache // (NZ * NC), cache // NC % NZ, cache % NC


def peer(cache, jz, jy, jc, sign):
    y, z, c = split_position(cache)
    ny = (y + NY + sign * signed(jy)) % NY
    nz = (z + NZ + sign * signed(jz)) % NZ
    nc = (c + jc) % NC
    return (ny * NZ + nz) * NC + nc


def slot_of(cache, owner):
    y, z, c = split_position(cache)
    oy, oz, oc = split_position(owner)
    dy, dz, dc = (oy - y + NY) % NY, (oz - z + NZ) % NZ, (oc - c + NC) % NC
    jy = jnp.where(dy == 0, 0, jnp.where(dy <= NY // 2, 2 * dy - 1, 2 * (NY - dy)))
    jz = jnp.where(dz == 0, 0, jnp.where(dz <= NZ // 2, 2 * dz - 1, 2 * (NZ - dz)))
    return (jz * NY + jy) * NC + dc


def iota(shape, dim):
    return lax.broadcasted_iota(jnp.int32, shape, dim)


def high_low(p):
    high = p.astype(jnp.bfloat16)
    low = (p - high.astype(jnp.float32)).astype(jnp.bfloat16)
    return jnp.concatenate([high, low], axis=0)


def dot_t(a, b):
    return lax.dot_general(a, b, (((1,), (1,)), ((), ())), preferred_element_type=jnp.float32)


def dot(a, b):
    return jnp.dot(a, b, preferred_element_type=jnp.float32)


def kernel(
    sel_ref, req_ref, q_ref, ck_ref, cv_ref, rk_ref, rv_ref, out_ref,
    ck, cv, rk, rv, rhs, msg_out, msg_in, res_out, res_in, near_out, near_in, far_o, far_s, slots,
    load_sem, msg_send, msg_recv, res_send, res_recv, near_send, near_recv,
):
    cache = lax.axis_index("cache")
    group = lax.axis_index("group")
    barrier = pltpu.get_barrier_semaphore()

    def each_peer(fn):
        def step(i, carry):
            j = PEERS - 1 - i
            fn(j, j // (NY * NC), j // NC % NY, j % NC)
            return carry

        lax.fori_loop(0, PEERS - 1, step, 0)

    def greet(j, jz, jy, jc):
        pl.semaphore_signal(
            barrier, inc=1, device_id=(peer(cache, jz, jy, jc, 1), group), device_id_type=MESH
        )

    each_peer(greet)
    for dg in range(1, NG):
        pl.semaphore_signal(
            barrier, inc=1, device_id=(cache, (group + dg) % NG), device_id_type=MESH
        )

    loads = [
        pltpu.make_async_copy(src, dst, load_sem.at[i])
        for i, (src, dst) in enumerate(((rk_ref, rk), (rv_ref, rv), (ck_ref, ck), (cv_ref, cv)))
    ]
    for load in loads:
        load.start()

    lane = iota((8, 128), 1)
    wanted_by = [jnp.full((8, 128), -1, jnp.int32) for _ in range(TOP)]
    codes = jnp.zeros((WANTED, 128), jnp.int32)
    code_row = iota((WANTED, 128), 0)
    for r in range(ROWS):
        prompt = req_ref[r]
        for h in range(HEADS):
            here = (lane < 32) & (lane // 16 == h) & (lane % 4 == r)
            for k in range(TOP):
                e = (r * HEADS + h) * TOP + k
                block = sel_ref[r, h, k]
                owner = block // 2
                slots[e] = slot_of(cache, owner)
                wanted_by[k] = jnp.where(here, owner, wanted_by[k])
                wanted_by[0] = jnp.where(lane == 32 + e, owner, wanted_by[0])
                codes = jnp.where(code_row == e, prompt * 4 + h * 2 + block % 2 + 1, codes)
    wanted_by = [jnp.broadcast_to(w[0:1], (64, 128)) for w in wanted_by]
    rhs[0:32, :] = q_ref[pl.ds(pl.multiple_of(group * 32, 32), 32), :]
    rhs[32:64, :] = codes.astype(jnp.float32).astype(jnp.bfloat16)
    rhs[64:128, :] = jnp.zeros((64, 128), jnp.bfloat16)
    table = rhs[...]
    row64 = iota((64, 128), 0)
    lane64 = iota((64, 128), 1)
    col_row = jnp.where(lane64 < 32, lane64 // 4 % 4, jnp.where(lane64 < 64, 4, 9))
    row_match = row64 % 8 == col_row
    y, z, c = split_position(cache)
    local = row64 // 8
    jy, jc = local // NC, local % NC
    vy = (y + NY + signed(jy)) % NY
    vc = (c + jc) % NC
    base = vy * (NZ * NC) + vc
    for jz in range(NZ):
        owner = base + ((z + NZ + signed(jz)) % NZ) * NC
        hit = wanted_by[0] == owner
        for k in range(1, TOP):
            hit = hit | (wanted_by[k] == owner)
        pick = jnp.where(hit & row_match, 1.0, 0.0).astype(jnp.bfloat16)
        msg_out[jz * 8 : (jz + 1) * 8] = dot(pick, table).reshape(8, 8, 128).astype(jnp.bfloat16)

    pl.semaphore_wait(barrier, PEERS - 1 + NG - 1)

    def message(j, jz, jy, jc):
        return pltpu.make_async_remote_copy(
            src_ref=msg_out.at[j, pl.ds(0, MSG)],
            dst_ref=msg_in.at[j, pl.ds(0, MSG)],
            send_sem=msg_send.at[j],
            recv_sem=msg_recv.at[j],
            device_id=(peer(cache, jz, jy, jc, 1), group),
            device_id_type=MESH,
        )

    each_peer(lambda *at: message(*at).start())
    own_message = pltpu.make_async_copy(
        msg_out.at[0, pl.ds(0, MSG)], msg_in.at[0, pl.ds(0, MSG)], msg_recv.at[0]
    )
    own_message.start()

    loads[0].wait()
    loads[1].wait()
    row16 = iota((16, RECENT), 0) % ROWS
    row32 = iota((32, HD), 0) % ROWS
    lane16 = iota((16, HD), 1)

    def recent(h, carry):
        x = q_ref[pl.ds(pl.multiple_of(h * 16, 16), 16), :]
        s = dot_t(x, rk[h])
        for r in range(1, ROWS):
            s = jnp.where(row16 == r, dot_t(x, rk[r * KVH + h]), s)
        s = s * SCALE
        m = jnp.max(s, axis=1, keepdims=True)
        p = jnp.exp(s - m)
        total = jnp.sum(p, axis=1, keepdims=True)
        both = high_low(p)
        o = dot(both, rv[h])
        for r in range(1, ROWS):
            o = jnp.where(row32 == r, dot(both, rv[r * KVH + h]), o)
        near_out[h, 0] = o[0:16] + o[16:32]
        near_out[h, 1] = jnp.where(lane16 < 64, m, total)
        return carry

    lax.fori_loop(0, KVH, recent, 0)

    nears = []
    for dg in range(1, NG):
        target = (group + dg) % NG
        nears.append(
            pltpu.make_async_remote_copy(
                src_ref=near_out.at[pl.ds(target * HEADS, HEADS)],
                dst_ref=near_in.at[dg],
                send_sem=near_send.at[dg],
                recv_sem=near_recv.at[dg],
                device_id=(cache, target),
                device_id_type=MESH,
            )
        )
    for near in nears:
        near.start()

    loads[2].wait()
    loads[3].wait()

    def result(j, jz, jy, jc):
        return pltpu.make_async_remote_copy(
            src_ref=res_out.at[j, pl.ds(0, RES)],
            dst_ref=res_in.at[j, pl.ds(0, RES)],
            send_sem=res_send.at[j],
            recv_sem=res_recv.at[j],
            device_id=(peer(cache, jz, jy, jc, -1), group),
            device_id_type=MESH,
        )

    own_result = pltpu.make_async_copy(
        res_out.at[0, pl.ds(0, RES)], res_in.at[0, pl.ds(0, RES)], res_recv.at[0]
    )
    row8 = iota((8, 128), 0)
    m_at = (lane == row8) & (row8 < PER_KV)
    t_at = (lane == row8 + PER_KV) & (row8 < PER_KV)

    def attend(j):
        x = msg_in[j]
        code = jnp.max(x[4:5, :].astype(jnp.float32)).astype(jnp.int32)
        block = jnp.clip(code - 1, 0, PEERS - 1)
        s = dot_t(x, ck[block]) * SCALE
        m = jnp.max(s, axis=1, keepdims=True)
        p = jnp.exp(s - m)
        total = jnp.sum(p, axis=1, keepdims=True)
        o = dot(high_low(p), cv[block])
        stat = jnp.sum(jnp.where(m_at, m, jnp.where(t_at, total, 0.0)), axis=0, keepdims=True)
        res_out[j] = jnp.where(row8 < PER_KV, o[0:8] + o[8:16], stat)

    def far(jz, first):
        for i in range(first, 8):
            message(jz * 8 + i, jz, i // NC, i % NC).wait_recv()
        if first:
            own_message.wait()
        for i in range(8):
            attend(jz * 8 + i)
        if first:
            own_result.start()
        for i in range(first, 8):
            result(jz * 8 + i, jz, i // NC, i % NC).start()

    far(0, 1)
    lax.fori_loop(1, NZ, lambda jz, carry: (far(jz, 0), carry)[1], 0)

    for near in nears:
        near.wait()
    own_result.wait()
    each_peer(lambda *at: result(*at).wait_recv())

    for r in range(ROWS):
        for h in range(HEADS):
            for k in range(TOP):
                e = (r * HEADS + h) * TOP + k
                tile = res_in[slots[e]]
                rows = pl.ds(h * 16 + r, 4, stride=4)
                far_o[k, rows, :] = tile[0:4]
                far_s[k, rows, :] = jnp.broadcast_to(tile[4:5], (4, 128))
    lane32 = iota((32, 128), 1)
    which = iota((32, 128), 0) // 4 % 4
    parts = []
    for k in range(TOP):
        stat = far_s[k]
        m = jnp.sum(jnp.where(lane32 == which, stat, 0.0), axis=1, keepdims=True)
        total = jnp.sum(jnp.where(lane32 == which + PER_KV, stat, 0.0), axis=1, keepdims=True)
        parts.append((far_o[k], m, total))
    for dg in range(NG):
        if dg:
            both = near_in[dg]
        else:
            both = near_out[pl.ds(group * HEADS, HEADS)]
        stat = both[:, 1].reshape(32, 128)
        parts.append((both[:, 0].reshape(32, 128), stat[:, 0:1], stat[:, 64:65]))
    peak = functools.reduce(jnp.maximum, [m for _, m, _ in parts])
    summed, weight = 0.0, 0.0
    for o, m, total in parts:
        factor = jnp.exp(m - peak)
        summed = summed + factor * o
        weight = weight + factor * total
    out_ref[...] = (summed / weight).astype(out_ref.dtype)

    each_peer(lambda *at: message(*at).wait_send())
    each_peer(lambda *at: result(*at).wait_send())


def per_device(queries, request_of, selected, cache_keys, cache_values, recent_keys, recent_values):
    q = queries.reshape(ROWS, KVH * PER_KV, HD).transpose(1, 0, 2).reshape(128, HD)
    blocks = lambda a: a.reshape(PEERS, BLOCK, HD)
    recents = lambda a: a.reshape(ROWS * KVH, RECENT, HD)
    vmem = lambda shape, kind: pltpu.VMEM(shape, kind)
    dma = pltpu.SemaphoreType.DMA
    bf16, f32 = jnp.bfloat16, jnp.float32
    out = pl.pallas_call(
        kernel,
        out_shape=jax.ShapeDtypeStruct((32, HD), bf16),
        in_specs=[pl.BlockSpec(memory_space=pltpu.SMEM)] * 2
        + [pl.BlockSpec(memory_space=pltpu.VMEM)]
        + [pl.BlockSpec(memory_space=pltpu.HBM)] * 4,
        out_specs=pl.BlockSpec(memory_space=pltpu.VMEM),
        scratch_shapes=[
            vmem((PEERS, BLOCK, HD), bf16),
            vmem((PEERS, BLOCK, HD), bf16),
            vmem((ROWS * KVH, RECENT, HD), bf16),
            vmem((ROWS * KVH, RECENT, HD), bf16),
            vmem((128, HD), bf16),
            vmem((PEERS, 8, HD), bf16),
            vmem((PEERS, 8, HD), bf16),
            vmem((PEERS, 8, HD), f32),
            vmem((PEERS, 8, HD), f32),
            vmem((KVH, 2, 16, HD), f32),
            vmem((NG, HEADS, 2, 16, HD), f32),
            vmem((TOP, 32, HD), f32),
            vmem((TOP, 32, HD), f32),
            pltpu.SMEM((WANTED,), jnp.int32),
            dma((4,)),
            dma((PEERS,)),
            dma((PEERS,)),
            dma((PEERS,)),
            dma((PEERS,)),
            dma((NG,)),
            dma((NG,)),
        ],
        compiler_params=pltpu.CompilerParams(
            collective_id=0, has_side_effects=True, vmem_limit_bytes=40 * 1024 * 1024
        ),
    )(
        selected, request_of, q, blocks(cache_keys), blocks(cache_values),
        recents(recent_keys), recents(recent_values),
    )
    return out.reshape(HEADS * PER_KV, ROWS, HD).transpose(1, 0, 2).reshape(ROWS, HEADS * PER_KV * HD)


def solution(mesh):
    return jax.shard_map(
        per_device,
        mesh=mesh,
        in_specs=(
            P("cache", None),
            P("cache"),
            P("cache", "group", None),
            P(None, "group", "cache", None),
            P(None, "group", "cache", None),
            P("cache", None, "group", None),
            P("cache", None, "group", None),
        ),
        out_specs=P("cache", "group"),
        check_vma=False,
    )
```

```python
import functools

import jax
import jax.numpy as jnp
from jax import lax
from jax.experimental import pallas as pl
from jax.experimental.pallas import tpu as pltpu
from jax.sharding import PartitionSpec as P

MESH = pl.DeviceIdType.MESH
NY, NZ, NC, NG = 4, 8, 2, 4
PEERS = NY * NZ * NC
ROWS, HEADS, PER_KV, TOP = 4, 2, 4, 4
KVH, HD, BLOCK = 8, 128, 128
RECENT = 256
SCALE = HD ** (-0.5)
MSG = 6
RES = 5
WANTED = ROWS * HEADS * TOP


def signed(j):
    return ((j + 1) // 2) * (2 * (j % 2) - 1)


def iota(shape, dim):
    return lax.broadcasted_iota(jnp.int32, shape, dim)


def high_low(p):
    high = p.astype(jnp.bfloat16)
    low = (p - high.astype(jnp.float32)).astype(jnp.bfloat16)
    return jnp.concatenate([high, low], axis=0)


def dot_t(a, b):
    return lax.dot_general(a, b, (((1,), (1,)), ((), ())), preferred_element_type=jnp.float32)


def dot(a, b):
    return jnp.dot(a, b, preferred_element_type=jnp.float32)


def kernel(
    sel_ref, req_ref, q_hbm, ck_ref, cv_ref, rk_ref, rv_ref, out_ref,
    q_ref, ck, cv, rk, rv, rhs, msg_out, msg_in, res_out, res_in, near_out, near_in, far_o, far_s,
    load_sem, msg_send, msg_recv, res_send, res_recv, near_send, near_recv,
):
    cache = lax.axis_index("cache")
    group = lax.axis_index("group")
    y = lax.div(cache, NZ * NC)
    z = lax.rem(lax.div(cache, NC), NZ)
    c = lax.rem(cache, NC)
    other_z = [lax.rem(z + (NZ + signed(jz)), NZ) * NC for jz in range(NZ)]
    other_y = [lax.rem(y + (NY + signed(jy)), NY) * (NZ * NC) for jy in range(NY)]
    other_c = [c, 1 - c]
    other_yc = [other_y[i // NC] + other_c[i % NC] for i in range(NY * NC)]
    opposite = lambda j, n: 0 if j == 0 else (j + 1 if j % 2 and j + 1 < n else j if j % 2 else j - 1)

    def ahead(j):
        return (other_z[j // 8] + other_yc[j % 8], group)

    def behind(j):
        jz, jy, jc = opposite(j // 8, NZ), opposite(j // NC % NY, NY), j % NC
        return (other_z[jz] + other_yc[jy * NC + jc], group)

    barrier = pltpu.get_barrier_semaphore()
    order = range(PEERS - 1, 0, -1)
    for j in order:
        pl.semaphore_signal(barrier, inc=1, device_id=ahead(j), device_id_type=MESH)
    for dg in range(1, NG):
        pl.semaphore_signal(
            barrier, inc=1, device_id=(cache, lax.rem(group + dg, NG)), device_id_type=MESH
        )

    loads = [
        pltpu.make_async_copy(src, dst, load_sem.at[i])
        for i, (src, dst) in enumerate(
            ((q_hbm, q_ref), (rk_ref, rk), (rv_ref, rv), (ck_ref, ck), (cv_ref, cv))
        )
    ]
    for load in loads:
        load.start()

    lane = iota((8, 128), 1)
    wanted_by = [jnp.full((8, 128), -1, jnp.int32) for _ in range(TOP)]
    codes = jnp.zeros((WANTED, 128), jnp.int32)
    code_row = iota((WANTED, 128), 0)
    for r in range(ROWS):
        prompt = req_ref[r]
        for h in range(HEADS):
            here = (lane < 32) & (lane // 16 == h) & (lane % 4 == r)
            for k in range(TOP):
                e = (r * HEADS + h) * TOP + k
                block = sel_ref[r, h, k]
                owner = lax.div(block, 2)
                wanted_by[k] = jnp.where(here, owner, wanted_by[k])
                wanted_by[0] = jnp.where(lane == 32 + e, owner, wanted_by[0])
                code = prompt * 4 + h * 2 + (block - owner * 2) + 1
                codes = jnp.where(code_row == e, code, codes)
    wanted_by = [jnp.broadcast_to(w[0:1], (64, 128)) for w in wanted_by]
    loads[0].wait()
    rhs[0:32, :] = q_ref[pl.ds(pl.multiple_of(group * 32, 32), 32), :]
    rhs[32:64, :] = codes.astype(jnp.float32).astype(jnp.bfloat16)
    rhs[64:128, :] = jnp.zeros((64, 128), jnp.bfloat16)
    table = rhs[...]
    row64 = iota((64, 128), 0)
    lane64 = iota((64, 128), 1)
    half = row64 // 8 % 2
    place = row64 % 8
    col_row = jnp.where(lane64 < 32, lane64 // 4 % 4 + 4 * half, jnp.where(lane64 < 64, 4 - half, 9))
    row_match = place == col_row
    base = jnp.zeros((64, 128), jnp.int32)
    for i in range(8):
        base = jnp.where(row64 // 8 == i, other_yc[i], base)
    for jz in range(NZ):
        owner = base + other_z[jz]
        hit = wanted_by[0] == owner
        for k in range(1, TOP):
            hit = hit | (wanted_by[k] == owner)
        pick = jnp.where(hit & row_match, 1.0, 0.0).astype(jnp.bfloat16)
        msg_out[jz * 8 : (jz + 1) * 8] = dot(pick, table).reshape(8, 8, 128).astype(jnp.bfloat16)

    pl.semaphore_wait(barrier, PEERS - 1 + NG - 1)

    def message(j):
        at = pl.ds(0, MSG) if j % 2 == 0 else pl.ds(8 - MSG, MSG)
        return pltpu.make_async_remote_copy(
            src_ref=msg_out.at[j, at],
            dst_ref=msg_in.at[j, at],
            send_sem=msg_send.at[j],
            recv_sem=msg_recv.at[j],
            device_id=ahead(j),
            device_id_type=MESH,
        )

    for j in order:
        message(j).start()
    own_message = pltpu.make_async_copy(
        msg_out.at[0, pl.ds(0, MSG)], msg_in.at[0, pl.ds(0, MSG)], msg_recv.at[0]
    )
    own_message.start()

    loads[1].wait()
    loads[2].wait()
    row16 = iota((16, RECENT), 0) % ROWS
    row32 = iota((32, HD), 0) % ROWS
    lane16 = iota((16, HD), 1)

    def recent(h, carry):
        x = q_ref[pl.ds(pl.multiple_of(h * 16, 16), 16), :]
        s = dot_t(x, rk[h])
        for r in range(1, ROWS):
            s = jnp.where(row16 == r, dot_t(x, rk[r * KVH + h]), s)
        s = s * SCALE
        m = jnp.max(s, axis=1, keepdims=True)
        p = jnp.exp(s - m)
        total = jnp.sum(p, axis=1, keepdims=True)
        both = high_low(p)
        o = dot(both, rv[h])
        for r in range(1, ROWS):
            o = jnp.where(row32 == r, dot(both, rv[r * KVH + h]), o)
        near_out[h, 0] = o[0:16] + o[16:32]
        near_out[h, 1] = jnp.where(lane16 < 64, m, total)
        return carry

    lax.fori_loop(0, KVH, recent, 0)

    nears = []
    for dg in range(1, NG):
        target = lax.rem(group + dg, NG)
        nears.append(
            pltpu.make_async_remote_copy(
                src_ref=near_out.at[pl.ds(target * HEADS, HEADS)],
                dst_ref=near_in.at[dg],
                send_sem=near_send.at[dg],
                recv_sem=near_recv.at[dg],
                device_id=(cache, target),
                device_id_type=MESH,
            )
        )
    for near in nears:
        near.start()

    loads[3].wait()
    loads[4].wait()

    def result(j):
        return pltpu.make_async_remote_copy(
            src_ref=res_out.at[j, pl.ds(0, RES)],
            dst_ref=res_in.at[j, pl.ds(0, RES)],
            send_sem=res_send.at[j],
            recv_sem=res_recv.at[j],
            device_id=behind(j),
            device_id_type=MESH,
        )

    own_result = pltpu.make_async_copy(
        res_out.at[0, pl.ds(0, RES)], res_in.at[0, pl.ds(0, RES)], res_recv.at[0]
    )
    row8 = iota((8, 128), 0)
    upper = row8 < PER_KV
    upper_x = iota((8, 128), 0) < PER_KV
    m_first = upper & (lane == row8)
    t_first = upper & (lane == row8 + PER_KV)
    m_second = (~upper) & (lane == row8 - PER_KV)
    t_second = (~upper) & (lane == row8)

    def block_of(x, row):
        code = x[row : row + 1, :].astype(jnp.float32)[0, 0].astype(jnp.int32)
        return jnp.clip(code - 1, 0, PEERS - 1)

    def far(jz):
        pairs = []
        for i in range(0, 8, 2):
            first, second = msg_in[jz * 8 + i], msg_in[jz * 8 + i + 1]
            a, b = block_of(first, 4), block_of(second, 3)
            x = jnp.where(upper_x, first.astype(jnp.float32), second.astype(jnp.float32))
            pairs.append((x.astype(jnp.bfloat16), a, b))
        scores = []
        for x, a, b in pairs:
            s = dot_t(x, jnp.concatenate([ck[a], ck[b]], axis=0))
            scores.append(jnp.where(upper, s[:, :BLOCK], s[:, BLOCK:]) * SCALE)
        highs = [jnp.max(s, axis=1, keepdims=True) for s in scores]
        weights = [jnp.exp(s - m) for s, m in zip(scores, highs)]
        totals = [jnp.sum(p, axis=1, keepdims=True) for p in weights]
        for n, ((x, a, b), p, m, t) in enumerate(zip(pairs, weights, highs, totals)):
            both = high_low(
                jnp.concatenate([jnp.where(upper, p, 0.0), jnp.where(upper, 0.0, p)], axis=1)
            )
            o = dot(both, jnp.concatenate([cv[a], cv[b]], axis=0))
            o = o[0:8] + o[8:16]
            one = jnp.sum(jnp.where(m_first, m, jnp.where(t_first, t, 0.0)), axis=0, keepdims=True)
            two = jnp.sum(jnp.where(m_second, m, jnp.where(t_second, t, 0.0)), axis=0, keepdims=True)
            res_out[jz * 8 + 2 * n] = jnp.where(upper, o, one)
            res_out[jz * 8 + 2 * n + 1] = jnp.where(upper, pltpu.roll(o, PER_KV, 0), two)

    for jz in range(NZ):
        for i in range(8):
            if jz + i:
                message(jz * 8 + i).wait_recv()
            else:
                own_message.wait()
        far(jz)
        for i in range(8):
            if jz + i:
                result(jz * 8 + i).start()
            else:
                own_result.start()

    slots = []
    for r in range(ROWS):
        for h in range(HEADS):
            for k in range(TOP):
                owner = lax.div(sel_ref[r, h, k], 2)
                oy = lax.div(owner, NZ * NC)
                oz = lax.rem(lax.div(owner, NC), NZ)
                dc = lax.rem(owner + c, NC)
                dy, dz = lax.rem(oy - y + NY, NY), lax.rem(oz - z + NZ, NZ)
                jy = jnp.where(dy == 0, 0, jnp.where(dy <= NY // 2, 2 * dy - 1, 2 * (NY - dy)))
                jz = jnp.where(dz == 0, 0, jnp.where(dz <= NZ // 2, 2 * dz - 1, 2 * (NZ - dz)))
                slots.append((jz * NY + jy) * NC + dc)

    for near in nears:
        near.wait()
    own_result.wait()
    for j in order:
        result(j).wait_recv()

    for r in range(ROWS):
        for h in range(HEADS):
            for k in range(TOP):
                e = (r * HEADS + h) * TOP + k
                tile = res_in[slots[e]]
                rows = pl.ds(h * 16 + r, 4, stride=4)
                far_o[k, rows, :] = tile[0:4]
                far_s[k, rows, :] = jnp.broadcast_to(tile[4:5], (4, 128))
    lane32 = iota((32, 128), 1)
    which = iota((32, 128), 0) // 4 % 4
    parts = []
    for k in range(TOP):
        stat = far_s[k]
        m = jnp.sum(jnp.where(lane32 == which, stat, 0.0), axis=1, keepdims=True)
        total = jnp.sum(jnp.where(lane32 == which + PER_KV, stat, 0.0), axis=1, keepdims=True)
        parts.append((far_o[k], m, total))
    for dg in range(NG):
        if dg:
            both = near_in[dg]
        else:
            both = near_out[pl.ds(group * HEADS, HEADS)]
        stat = both[:, 1].reshape(32, 128)
        parts.append((both[:, 0].reshape(32, 128), stat[:, 0:1], stat[:, 64:65]))
    peak = functools.reduce(jnp.maximum, [m for _, m, _ in parts])
    summed, weight = 0.0, 0.0
    for o, m, total in parts:
        factor = jnp.exp(m - peak)
        summed = summed + factor * o
        weight = weight + factor * total
    out_ref[...] = (summed / weight).astype(out_ref.dtype)

    for j in order:
        message(j).wait_send()
    for j in order:
        result(j).wait_send()


def per_device(queries, request_of, selected, cache_keys, cache_values, recent_keys, recent_values):
    q = queries.reshape(ROWS, KVH * PER_KV, HD).transpose(1, 0, 2).reshape(128, HD)
    blocks = lambda a: a.reshape(PEERS, BLOCK, HD)
    recents = lambda a: a.reshape(ROWS * KVH, RECENT, HD)
    vmem = lambda shape, kind: pltpu.VMEM(shape, kind)
    dma = pltpu.SemaphoreType.DMA
    bf16, f32 = jnp.bfloat16, jnp.float32
    out = pl.pallas_call(
        kernel,
        out_shape=jax.ShapeDtypeStruct((32, HD), bf16),
        in_specs=[pl.BlockSpec(memory_space=pltpu.SMEM)] * 2
        + [pl.BlockSpec(memory_space=pltpu.HBM)] * 5,
        out_specs=pl.BlockSpec(memory_space=pltpu.VMEM),
        scratch_shapes=[
            vmem((128, HD), bf16),
            vmem((PEERS, BLOCK, HD), bf16),
            vmem((PEERS, BLOCK, HD), bf16),
            vmem((ROWS * KVH, RECENT, HD), bf16),
            vmem((ROWS * KVH, RECENT, HD), bf16),
            vmem((128, HD), bf16),
            vmem((PEERS, 8, HD), bf16),
            vmem((PEERS, 8, HD), bf16),
            vmem((PEERS, 8, HD), f32),
            vmem((PEERS, 8, HD), f32),
            vmem((KVH, 2, 16, HD), f32),
            vmem((NG, HEADS, 2, 16, HD), f32),
            vmem((TOP, 32, HD), f32),
            vmem((TOP, 32, HD), f32),
            dma((5,)),
            dma((PEERS,)),
            dma((PEERS,)),
            dma((PEERS,)),
            dma((PEERS,)),
            dma((NG,)),
            dma((NG,)),
        ],
        compiler_params=pltpu.CompilerParams(
            collective_id=0, has_side_effects=True, vmem_limit_bytes=67043328
        ),
    )(
        selected, request_of, q, blocks(cache_keys), blocks(cache_values),
        recents(recent_keys), recents(recent_values),
    )
    return out.reshape(HEADS * PER_KV, ROWS, HD).transpose(1, 0, 2).reshape(ROWS, HEADS * PER_KV * HD)


def solution(mesh):
    return jax.shard_map(
        per_device,
        mesh=mesh,
        in_specs=(
            P("cache", None),
            P("cache"),
            P("cache", "group", None),
            P(None, "group", "cache", None),
            P(None, "group", "cache", None),
            P("cache", None, "group", None),
            P("cache", None, "group", None),
        ),
        out_specs=P("cache", "group"),
        check_vma=False,
    )
```

```python
import functools

import jax
import jax.numpy as jnp
from jax import lax
from jax.experimental import pallas as pl
from jax.experimental.pallas import tpu as pltpu
from jax.sharding import PartitionSpec as P

MESH = pl.DeviceIdType.MESH
NY, NZ, NC, NG = 4, 8, 2, 4
PEERS = NY * NZ * NC
ROWS, HEADS, PER_KV, TOP = 4, 2, 4, 4
KVH, HD, BLOCK = 8, 128, 128
RECENT = 256
SCALE = HD ** (-0.5)
MSG = 6
RES = 5
WANTED = ROWS * HEADS * TOP


def signed(j):
    return ((j + 1) // 2) * (2 * (j % 2) - 1)


def iota(shape, dim):
    return lax.broadcasted_iota(jnp.int32, shape, dim)


def high_low(p):
    high = p.astype(jnp.bfloat16)
    low = (p - high.astype(jnp.float32)).astype(jnp.bfloat16)
    return jnp.concatenate([high, low], axis=0)


def dot_t(a, b):
    return lax.dot_general(a, b, (((1,), (1,)), ((), ())), preferred_element_type=jnp.float32)


def dot(a, b):
    return jnp.dot(a, b, preferred_element_type=jnp.float32)


def kernel(
    sel_hbm, req_hbm, q_hbm, ck_ref, cv_ref, rk_ref, rv_ref, out_hbm,
    sel_ref, req_ref, out_ref, q_ref, ck, cv, rk, rv, rhs, msg_out, msg_in, res_out, res_in, near_out, near_in, far_o, far_s,
    load_sem, out_sem, msg_send, msg_recv, res_send, res_recv, near_send, near_recv,
):
    cache = lax.axis_index("cache")
    group = lax.axis_index("group")
    y = lax.div(cache, NZ * NC)
    z = lax.rem(lax.div(cache, NC), NZ)
    c = lax.rem(cache, NC)
    other_z = [lax.rem(z + (NZ + signed(jz)), NZ) * NC for jz in range(NZ)]
    other_y = [lax.rem(y + (NY + signed(jy)), NY) * (NZ * NC) for jy in range(NY)]
    other_c = [c, 1 - c]
    other_yc = [other_y[i // NC] + other_c[i % NC] for i in range(NY * NC)]
    opposite = lambda j, n: 0 if j == 0 else (j + 1 if j % 2 and j + 1 < n else j if j % 2 else j - 1)

    def ahead(j):
        return (other_z[j // 8] + other_yc[j % 8], group)

    def behind(j):
        jz, jy, jc = opposite(j // 8, NZ), opposite(j // NC % NY, NY), j % NC
        return (other_z[jz] + other_yc[jy * NC + jc], group)

    barrier = pltpu.get_barrier_semaphore()
    order = range(PEERS - 1, 0, -1)
    for j in order:
        pl.semaphore_signal(barrier, inc=1, device_id=ahead(j), device_id_type=MESH)
    for dg in range(1, NG):
        pl.semaphore_signal(
            barrier, inc=1, device_id=(cache, lax.rem(group + dg, NG)), device_id_type=MESH
        )

    loads = [
        pltpu.make_async_copy(src, dst, load_sem.at[i])
        for i, (src, dst) in enumerate(
            (
                (sel_hbm, sel_ref), (req_hbm, req_ref), (q_hbm, q_ref),
                (rk_ref, rk), (rv_ref, rv), (ck_ref, ck), (cv_ref, cv),
            )
        )
    ]
    for load in loads:
        load.start()

    loads[0].wait()
    loads[1].wait()

    lane = iota((8, 128), 1)
    wanted_by = [jnp.full((8, 128), -1, jnp.int32) for _ in range(TOP)]
    codes = jnp.zeros((WANTED, 128), jnp.int32)
    code_row = iota((WANTED, 128), 0)
    for r in range(ROWS):
        prompt = req_ref[r]
        for h in range(HEADS):
            here = (lane < 32) & (lane // 16 == h) & (lane % 4 == r)
            for k in range(TOP):
                e = (r * HEADS + h) * TOP + k
                block = sel_ref[r, h, k]
                owner = lax.div(block, 2)
                wanted_by[k] = jnp.where(here, owner, wanted_by[k])
                wanted_by[0] = jnp.where(lane == 32 + e, owner, wanted_by[0])
                code = prompt * 4 + h * 2 + (block - owner * 2) + 1
                codes = jnp.where(code_row == e, code, codes)
    wanted_by = [jnp.broadcast_to(w[0:1], (64, 128)) for w in wanted_by]
    loads[2].wait()
    rhs[0:32, :] = q_ref[pl.ds(pl.multiple_of(group * 32, 32), 32), :]
    rhs[32:64, :] = codes.astype(jnp.float32).astype(jnp.bfloat16)
    rhs[64:128, :] = jnp.zeros((64, 128), jnp.bfloat16)
    table = rhs[...]
    row64 = iota((64, 128), 0)
    lane64 = iota((64, 128), 1)
    half = row64 // 8 % 2
    place = row64 % 8
    col_row = jnp.where(lane64 < 32, lane64 // 4 % 4 + 4 * half, jnp.where(lane64 < 64, 4 - half, 9))
    row_match = place == col_row
    base = jnp.zeros((64, 128), jnp.int32)
    for i in range(8):
        base = jnp.where(row64 // 8 == i, other_yc[i], base)
    for jz in range(NZ):
        owner = base + other_z[jz]
        hit = wanted_by[0] == owner
        for k in range(1, TOP):
            hit = hit | (wanted_by[k] == owner)
        pick = jnp.where(hit & row_match, 1.0, 0.0).astype(jnp.bfloat16)
        msg_out[jz * 8 : (jz + 1) * 8] = dot(pick, table).reshape(8, 8, 128).astype(jnp.bfloat16)

    pl.semaphore_wait(barrier, PEERS - 1 + NG - 1)

    def message(j):
        at = pl.ds(0, MSG) if j % 2 == 0 else pl.ds(8 - MSG, MSG)
        return pltpu.make_async_remote_copy(
            src_ref=msg_out.at[j, at],
            dst_ref=msg_in.at[j, at],
            send_sem=msg_send,
            recv_sem=msg_recv.at[j // 8],
            device_id=ahead(j),
            device_id_type=MESH,
        )

    for j in order:
        message(j).start()
    own_message = pltpu.make_async_copy(
        msg_out.at[0, pl.ds(0, MSG)], msg_in.at[0, pl.ds(0, MSG)], msg_recv.at[0]
    )
    own_message.start()

    slots = []
    for r in range(ROWS):
        for h in range(HEADS):
            for k in range(TOP):
                owner = lax.div(sel_ref[r, h, k], 2)
                oy = lax.div(owner, NZ * NC)
                oz = lax.rem(lax.div(owner, NC), NZ)
                dc = lax.rem(owner + c, NC)
                dy, dz = lax.rem(oy - y + NY, NY), lax.rem(oz - z + NZ, NZ)
                jy = jnp.where(dy == 0, 0, jnp.where(dy <= NY // 2, 2 * dy - 1, 2 * (NY - dy)))
                jz = jnp.where(dz == 0, 0, jnp.where(dz <= NZ // 2, 2 * dz - 1, 2 * (NZ - dz)))
                slots.append((jz * NY + jy) * NC + dc)

    loads[3].wait()
    loads[4].wait()
    row16 = iota((16, RECENT), 0) % ROWS
    row32 = iota((32, HD), 0) % ROWS
    lane16 = iota((16, HD), 1)

    def recent(h, carry):
        x = q_ref[pl.ds(pl.multiple_of(h * 16, 16), 16), :]
        s = dot_t(x, rk[h])
        for r in range(1, ROWS):
            s = jnp.where(row16 == r, dot_t(x, rk[r * KVH + h]), s)
        s = s * SCALE
        m = jnp.max(s, axis=1, keepdims=True)
        p = jnp.exp(s - m)
        total = jnp.sum(p, axis=1, keepdims=True)
        both = high_low(p)
        o = dot(both, rv[h])
        for r in range(1, ROWS):
            o = jnp.where(row32 == r, dot(both, rv[r * KVH + h]), o)
        near_out[h, 0] = o[0:16] + o[16:32]
        near_out[h, 1] = jnp.where(lane16 < 64, m, total)
        return carry

    lax.fori_loop(0, KVH, recent, 0)

    nears = []
    for dg in range(1, NG):
        target = lax.rem(group + dg, NG)
        nears.append(
            pltpu.make_async_remote_copy(
                src_ref=near_out.at[pl.ds(target * HEADS, HEADS)],
                dst_ref=near_in.at[dg],
                send_sem=near_send.at[dg],
                recv_sem=near_recv.at[dg],
                device_id=(cache, target),
                device_id_type=MESH,
            )
        )
    for near in nears:
        near.start()

    loads[5].wait()
    loads[6].wait()

    def result(j):
        return pltpu.make_async_remote_copy(
            src_ref=res_out.at[j, pl.ds(0, RES)],
            dst_ref=res_in.at[j, pl.ds(0, RES)],
            send_sem=res_send,
            recv_sem=res_recv,
            device_id=behind(j),
            device_id_type=MESH,
        )

    own_result = pltpu.make_async_copy(
        res_out.at[0, pl.ds(0, RES)], res_in.at[0, pl.ds(0, RES)], res_recv
    )
    row8 = iota((8, 128), 0)
    upper = row8 < PER_KV
    m_first = upper & (lane == row8)
    t_first = upper & (lane == row8 + PER_KV)
    m_second = (~upper) & (lane == row8 - PER_KV)
    t_second = (~upper) & (lane == row8)

    def block_of(x, row):
        code = x[row : row + 1, :].astype(jnp.float32)[0, 0].astype(jnp.int32)
        return jnp.clip(code - 1, 0, PEERS - 1)

    def scores_of(jz):
        msgs = pl.ds(jz * 8, 8)
        pltpu.make_async_copy(
            msg_out.at[msgs, pl.ds(0, MSG)], msg_in.at[msgs, pl.ds(0, MSG)], msg_recv.at[jz]
        ).wait()
        pairs = []
        for i in range(0, 8, 2):
            first, second = msg_in[jz * 8 + i], msg_in[jz * 8 + i + 1]
            a, b = block_of(first, 4), block_of(second, 3)
            x = jnp.where(upper, first.astype(jnp.float32), second.astype(jnp.float32))
            pairs.append((x.astype(jnp.bfloat16), a, b))
        out = []
        for x, a, b in pairs:
            s = dot_t(x, jnp.concatenate([ck[a], ck[b]], axis=0))
            out.append((jnp.where(upper, s[:, :BLOCK], s[:, BLOCK:]) * SCALE, a, b))
        return out

    def weights_of(scores):
        highs = [jnp.max(s, axis=1, keepdims=True) for s, _, _ in scores]
        return [(jnp.exp(s - m), m, a, b) for (s, a, b), m in zip(scores, highs)]

    def send_back(jz, weights):
        totals = [jnp.sum(p, axis=1, keepdims=True) for p, _, _, _ in weights]
        for n, ((p, m, a, b), t) in enumerate(zip(weights, totals)):
            both = high_low(
                jnp.concatenate([jnp.where(upper, p, 0.0), jnp.where(upper, 0.0, p)], axis=1)
            )
            o = dot(both, jnp.concatenate([cv[a], cv[b]], axis=0))
            o = o[0:8] + o[8:16]
            one = jnp.sum(jnp.where(m_first, m, jnp.where(t_first, t, 0.0)), axis=0, keepdims=True)
            two = jnp.sum(jnp.where(m_second, m, jnp.where(t_second, t, 0.0)), axis=0, keepdims=True)
            res_out[jz * 8 + 2 * n] = jnp.where(upper, o, one)
            res_out[jz * 8 + 2 * n + 1] = jnp.where(upper, pltpu.roll(o, PER_KV, 0), two)
        for i in range(8):
            if jz + i:
                result(jz * 8 + i).start()
            else:
                own_result.start()

    scores, weights = {}, {}
    for step in range(NZ + 2):
        if step < NZ:
            scores[step] = scores_of(step)
        if 0 <= step - 1 < NZ:
            weights[step - 1] = weights_of(scores[step - 1])
        if 0 <= step - 2:
            send_back(step - 2, weights[step - 2])

    for near in nears:
        near.wait()
    returned = pl.ds(0, RES)
    pltpu.make_async_copy(res_out.at[:, returned], res_in.at[:, returned], res_recv).wait()

    for r in range(ROWS):
        for h in range(HEADS):
            for k in range(TOP):
                e = (r * HEADS + h) * TOP + k
                tile = res_in[slots[e]]
                rows = pl.ds(h * 16 + r, 4, stride=4)
                far_o[k, rows, :] = tile[0:4]
                far_s[k, rows, :] = jnp.broadcast_to(tile[4:5], (4, 128))
    lane32 = iota((32, 128), 1)
    which = iota((32, 128), 0) // 4 % 4
    parts = []
    for k in range(TOP):
        stat = far_s[k]
        m = jnp.sum(jnp.where(lane32 == which, stat, 0.0), axis=1, keepdims=True)
        total = jnp.sum(jnp.where(lane32 == which + PER_KV, stat, 0.0), axis=1, keepdims=True)
        parts.append((far_o[k], m, total))
    for dg in range(NG):
        if dg:
            both = near_in[dg]
        else:
            both = near_out[pl.ds(group * HEADS, HEADS)]
        stat = both[:, 1].reshape(32, 128)
        parts.append((both[:, 0].reshape(32, 128), stat[:, 0:1], stat[:, 64:65]))
    peak = functools.reduce(jnp.maximum, [m for _, m, _ in parts])
    summed, weight = 0.0, 0.0
    for o, m, total in parts:
        factor = jnp.exp(m - peak)
        summed = summed + factor * o
        weight = weight + factor * total
    out_ref[...] = (summed / weight).astype(out_ref.dtype)

    write = pltpu.make_async_copy(out_ref, out_hbm, out_sem)
    write.start()
    others = pl.ds(1, PEERS - 1)
    for buffer, rows, sem in ((msg_out, MSG, msg_send), (res_out, RES, res_send)):
        sent = buffer.at[others, pl.ds(0, rows)]
        pltpu.make_async_copy(sent, sent, sem).wait()
    write.wait()


def per_device(queries, request_of, selected, cache_keys, cache_values, recent_keys, recent_values):
    q = queries.reshape(ROWS, KVH * PER_KV, HD).transpose(1, 0, 2).reshape(128, HD)
    blocks = lambda a: a.reshape(PEERS, BLOCK, HD)
    recents = lambda a: a.reshape(ROWS * KVH, RECENT, HD)
    vmem = lambda shape, kind: pltpu.VMEM(shape, kind)
    dma = pltpu.SemaphoreType.DMA
    bf16, f32 = jnp.bfloat16, jnp.float32
    out = pl.pallas_call(
        kernel,
        out_shape=jax.ShapeDtypeStruct((32, HD), bf16),
        in_specs=[pl.BlockSpec(memory_space=pltpu.HBM)] * 7,
        out_specs=pl.BlockSpec(memory_space=pltpu.HBM),
        scratch_shapes=[
            pltpu.SMEM((ROWS, HEADS, TOP), jnp.int32),
            pltpu.SMEM((ROWS,), jnp.int32),
            vmem((32, HD), bf16),
            vmem((128, HD), bf16),
            vmem((PEERS, BLOCK, HD), bf16),
            vmem((PEERS, BLOCK, HD), bf16),
            vmem((ROWS * KVH, RECENT, HD), bf16),
            vmem((ROWS * KVH, RECENT, HD), bf16),
            vmem((128, HD), bf16),
            vmem((PEERS, 8, HD), bf16),
            vmem((PEERS, 8, HD), bf16),
            vmem((PEERS, 8, HD), f32),
            vmem((PEERS, 8, HD), f32),
            vmem((KVH, 2, 16, HD), f32),
            vmem((NG, HEADS, 2, 16, HD), f32),
            vmem((TOP, 32, HD), f32),
            vmem((TOP, 32, HD), f32),
            dma((7,)),
            dma,
            dma,
            dma((NZ,)),
            dma,
            dma,
            dma((NG,)),
            dma((NG,)),
        ],
        compiler_params=pltpu.CompilerParams(
            collective_id=0, has_side_effects=True, vmem_limit_bytes=67043328
        ),
    )(
        selected, request_of, q, blocks(cache_keys), blocks(cache_values),
        recents(recent_keys), recents(recent_values),
    )
    return out.reshape(HEADS * PER_KV, ROWS, HD).transpose(1, 0, 2).reshape(ROWS, HEADS * PER_KV * HD)


def solution(mesh):
    return jax.shard_map(
        per_device,
        mesh=mesh,
        in_specs=(
            P("cache", None),
            P("cache"),
            P("cache", "group", None),
            P(None, "group", "cache", None),
            P(None, "group", "cache", None),
            P("cache", None, "group", None),
            P("cache", None, "group", None),
        ),
        out_specs=P("cache", "group"),
        check_vma=False,
    )
```

```python
import functools

import jax
import jax.numpy as jnp
from jax import lax
from jax.experimental import pallas as pl
from jax.experimental.pallas import tpu as pltpu
from jax.sharding import PartitionSpec as P

MESH = pl.DeviceIdType.MESH
NY, NZ, NC, NG = 4, 8, 2, 4
PEERS = NY * NZ * NC
ROWS, HEADS, PER_KV, TOP = 4, 2, 4, 4
KVH, HD, BLOCK = 8, 128, 128
RECENT = 256
SCALE = HD ** (-0.5)
MSG = 6
RES = 5
AHEAD = 2
WANTED = ROWS * HEADS * TOP


def signed(j):
    return ((j + 1) // 2) * (2 * (j % 2) - 1)


def hops(chip):
    return abs(signed(chip // NY)) + abs(signed(chip % NY))


CHIPS = sorted(range(NY * NZ), key=hops)
WAVES = [[chip for chip in CHIPS if hops(chip) in at] for at in ((0, 1), (2,), (3,), (4,), (5,), (6,))]
WAVE_OF = {chip: n for n, wave in enumerate(WAVES) for chip in wave}


def iota(shape, dim):
    return lax.broadcasted_iota(jnp.int32, shape, dim)


def high_low(p):
    high = p.astype(jnp.bfloat16)
    low = (p - high.astype(jnp.float32)).astype(jnp.bfloat16)
    return jnp.concatenate([high, low], axis=0)


def dot_t(a, b):
    return lax.dot_general(a, b, (((1,), (1,)), ((), ())), preferred_element_type=jnp.float32)


def dot(a, b):
    return jnp.dot(a, b, preferred_element_type=jnp.float32)


def kernel(
    sel_hbm, req_hbm, q_hbm, ck_ref, cv_ref, rk_ref, rv_ref, out_hbm,
    sel_ref, req_ref, out_ref, q_ref, ck, cv, rk, rv, rhs, msg_out, msg_in, res_out, res_in, near_out, near_in, far_o, far_s,
    load_sem, out_sem, msg_send, msg_recv, res_send, res_recv, near_send, near_recv,
):
    cache = lax.axis_index("cache")
    group = lax.axis_index("group")
    y = lax.div(cache, NZ * NC)
    z = lax.rem(lax.div(cache, NC), NZ)
    c = lax.rem(cache, NC)
    other_z = [lax.rem(z + (NZ + signed(jz)), NZ) * NC for jz in range(NZ)]
    other_y = [lax.rem(y + (NY + signed(jy)), NY) * (NZ * NC) for jy in range(NY)]
    other_c = [c, 1 - c]
    other_yc = [other_y[i // NC] + other_c[i % NC] for i in range(NY * NC)]
    opposite = lambda j, n: 0 if j == 0 else (j + 1 if j % 2 and j + 1 < n else j if j % 2 else j - 1)

    def ahead(j):
        return (other_z[j // 8] + other_yc[j % 8], group)

    def behind(j):
        jz, jy, jc = opposite(j // 8, NZ), opposite(j // NC % NY, NY), j % NC
        return (other_z[jz] + other_yc[jy * NC + jc], group)

    barrier = pltpu.get_barrier_semaphore()
    order = [2 * chip + i for chip in reversed(CHIPS) for i in (1, 0) if chip + i]
    for j in order:
        pl.semaphore_signal(barrier, inc=1, device_id=ahead(j), device_id_type=MESH)
    for dg in range(1, NG):
        pl.semaphore_signal(
            barrier, inc=1, device_id=(cache, lax.rem(group + dg, NG)), device_id_type=MESH
        )

    loads = [
        pltpu.make_async_copy(src, dst, load_sem.at[i])
        for i, (src, dst) in enumerate(
            (
                (sel_hbm, sel_ref), (req_hbm, req_ref), (q_hbm, q_ref),
                (rk_ref, rk), (rv_ref, rv), (ck_ref, ck), (cv_ref, cv),
            )
        )
    ]
    for load in loads:
        load.start()

    loads[0].wait()
    loads[1].wait()

    lane = iota((8, 128), 1)
    wanted_by = [jnp.full((8, 128), -1, jnp.int32) for _ in range(TOP)]
    codes = jnp.zeros((WANTED, 128), jnp.int32)
    code_row = iota((WANTED, 128), 0)
    for r in range(ROWS):
        prompt = req_ref[r]
        for h in range(HEADS):
            here = (lane < 32) & (lane // 16 == h) & (lane % 4 == r)
            for k in range(TOP):
                e = (r * HEADS + h) * TOP + k
                block = sel_ref[r, h, k]
                owner = lax.shift_right_logical(block, 1)
                wanted_by[k] = jnp.where(here, owner, wanted_by[k])
                wanted_by[0] = jnp.where(lane == 32 + e, owner, wanted_by[0])
                code = prompt * 4 + h * 2 + (block - owner * 2) + 1
                codes = jnp.where(code_row == e, code, codes)
    wanted_by = [jnp.broadcast_to(w[0:1], (64, 128)) for w in wanted_by]
    loads[2].wait()
    rhs[0:32, :] = q_ref[pl.ds(pl.multiple_of(group * 32, 32), 32), :]
    rhs[32:64, :] = codes.astype(jnp.float32).astype(jnp.bfloat16)
    rhs[64:128, :] = jnp.zeros((64, 128), jnp.bfloat16)
    table = rhs[...]
    row64 = iota((64, 128), 0)
    lane64 = iota((64, 128), 1)
    half = row64 // 8 % 2
    place = row64 % 8
    col_row = jnp.where(lane64 < 32, lane64 // 4 % 4 + 4 * half, jnp.where(lane64 < 64, 4 - half, 9))
    row_match = place == col_row
    base = jnp.zeros((64, 128), jnp.int32)
    for i in range(8):
        base = jnp.where(row64 // 8 == i, other_yc[i], base)
    for jz in range(NZ):
        owner = base + other_z[jz]
        hit = wanted_by[0] == owner
        for k in range(1, TOP):
            hit = hit | (wanted_by[k] == owner)
        pick = jnp.where(hit & row_match, 1.0, 0.0).astype(jnp.bfloat16)
        msg_out[jz * 8 : (jz + 1) * 8] = dot(pick, table).reshape(8, 8, 128).astype(jnp.bfloat16)

    pl.semaphore_wait(barrier, PEERS - 1 + NG - 1)

    def message(j):
        at = pl.ds(0, MSG) if j % 2 == 0 else pl.ds(8 - MSG, MSG)
        return pltpu.make_async_remote_copy(
            src_ref=msg_out.at[j, at],
            dst_ref=msg_in.at[j, at],
            send_sem=msg_send,
            recv_sem=msg_recv.at[WAVE_OF[j // 2]],
            device_id=ahead(j),
            device_id_type=MESH,
        )

    for j in order:
        message(j).start()
    own_message = pltpu.make_async_copy(
        msg_out.at[0, pl.ds(0, MSG)], msg_in.at[0, pl.ds(0, MSG)], msg_recv.at[0]
    )
    own_message.start()

    loads[3].wait()
    loads[4].wait()
    row16 = iota((16, RECENT), 0) % ROWS
    row32 = iota((32, HD), 0) % ROWS
    lane16 = iota((16, HD), 1)

    def recent_scores(h):
        x = q_ref[h * 16 : (h + 1) * 16, :]
        s = dot_t(x, rk[h])
        for r in range(1, ROWS):
            s = jnp.where(row16 == r, dot_t(x, rk[r * KVH + h]), s)
        return s * SCALE

    def recent_rest(h, s):
        m = jnp.max(s, axis=1, keepdims=True)
        p = jnp.exp(s - m)
        total = jnp.sum(p, axis=1, keepdims=True)
        both = high_low(p)
        o = dot(both, rv[h])
        for r in range(1, ROWS):
            o = jnp.where(row32 == r, dot(both, rv[r * KVH + h]), o)
        near_out[h, 0] = o[0:16] + o[16:32]
        near_out[h, 1] = jnp.where(lane16 < 64, m, total)

    pending = []
    for h in range(KVH):
        pending.append((h, recent_scores(h)))
        if h >= AHEAD:
            recent_rest(*pending.pop(0))
    for item in pending:
        recent_rest(*item)

    nears = []
    for dg in range(1, NG):
        target = lax.rem(group + dg, NG)
        nears.append(
            pltpu.make_async_remote_copy(
                src_ref=near_out.at[pl.ds(target * HEADS, HEADS)],
                dst_ref=near_in.at[dg],
                send_sem=near_send.at[dg],
                recv_sem=near_recv.at[dg],
                device_id=(cache, target),
                device_id_type=MESH,
            )
        )
    for near in nears:
        near.start()

    loads[5].wait()
    loads[6].wait()

    def result(j):
        return pltpu.make_async_remote_copy(
            src_ref=res_out.at[j, pl.ds(0, RES)],
            dst_ref=res_in.at[cache, pl.ds(0, RES)],
            send_sem=res_send,
            recv_sem=res_recv,
            device_id=behind(j),
            device_id_type=MESH,
        )

    own_result = pltpu.make_async_copy(
        res_out.at[0, pl.ds(0, RES)], res_in.at[cache, pl.ds(0, RES)], res_recv
    )
    row8 = iota((8, 128), 0)
    upper = row8 < PER_KV
    m_first = upper & (lane == row8)
    t_first = upper & (lane == row8 + PER_KV)
    m_second = (~upper) & (lane == row8 - PER_KV)
    t_second = (~upper) & (lane == row8)

    def block_of(x, row):
        code = x[row : row + 1, :].astype(jnp.float32)[0, 0].astype(jnp.int32)
        return jnp.clip(code - 1, 0, PEERS - 1)

    def far(n):
        wave = WAVES[n]
        arrived = msg_in.at[pl.ds(0, 2 * len(wave)), pl.ds(0, MSG)]
        pltpu.make_async_copy(arrived, arrived, msg_recv.at[n]).wait()
        pairs = []
        for chip in wave:
            first, second = msg_in[2 * chip], msg_in[2 * chip + 1]
            a, b = block_of(first, 4), block_of(second, 3)
            x = jnp.where(upper, first.astype(jnp.float32), second.astype(jnp.float32))
            pairs.append((x.astype(jnp.bfloat16), a, b))
        scores = []
        for x, a, b in pairs:
            s = dot_t(x, jnp.concatenate([ck[a], ck[b]], axis=0))
            scores.append(jnp.where(upper, s[:, :BLOCK], s[:, BLOCK:]) * SCALE)
        highs = [jnp.max(s, axis=1, keepdims=True) for s in scores]
        weights = [jnp.exp(s - m) for s, m in zip(scores, highs)]
        totals = [jnp.sum(p, axis=1, keepdims=True) for p in weights]
        for chip, (x, a, b), p, m, t in zip(wave, pairs, weights, highs, totals):
            both = high_low(
                jnp.concatenate([jnp.where(upper, p, 0.0), jnp.where(upper, 0.0, p)], axis=1)
            )
            o = dot(both, jnp.concatenate([cv[a], cv[b]], axis=0))
            o = o[0:8] + o[8:16]
            one = jnp.sum(jnp.where(m_first, m, jnp.where(t_first, t, 0.0)), axis=0, keepdims=True)
            two = jnp.sum(jnp.where(m_second, m, jnp.where(t_second, t, 0.0)), axis=0, keepdims=True)
            res_out[2 * chip] = jnp.where(upper, o, one)
            res_out[2 * chip + 1] = jnp.where(upper, pltpu.roll(o, PER_KV, 0), two)
        for chip in reversed(wave):
            for i in (1, 0):
                if chip + i:
                    result(2 * chip + i).start()
                else:
                    own_result.start()

    for n in range(len(WAVES)):
        far(n)

    for near in nears:
        near.wait()
    returned = pl.ds(0, RES)
    pltpu.make_async_copy(res_out.at[:, returned], res_in.at[:, returned], res_recv).wait()

    for r in range(ROWS):
        for h in range(HEADS):
            for k in range(TOP):
                tile = res_in[lax.shift_right_logical(sel_ref[r, h, k], 1)]
                rows = pl.ds(h * 16 + r, 4, stride=4)
                far_o[k, rows, :] = tile[0:4]
                far_s[k, rows, :] = jnp.broadcast_to(tile[4:5], (4, 128))
    lane32 = iota((32, 128), 1)
    which = iota((32, 128), 0) // 4 % 4
    parts = []
    for k in range(TOP):
        stat = far_s[k]
        m = jnp.sum(jnp.where(lane32 == which, stat, 0.0), axis=1, keepdims=True)
        total = jnp.sum(jnp.where(lane32 == which + PER_KV, stat, 0.0), axis=1, keepdims=True)
        parts.append((far_o[k], m, total))
    for dg in range(NG):
        if dg:
            both = near_in[dg]
        else:
            both = near_out[pl.ds(group * HEADS, HEADS)]
        stat = both[:, 1].reshape(32, 128)
        parts.append((both[:, 0].reshape(32, 128), stat[:, 0:1], stat[:, 64:65]))
    peak = functools.reduce(jnp.maximum, [m for _, m, _ in parts])
    summed, weight = 0.0, 0.0
    for o, m, total in parts:
        factor = jnp.exp(m - peak)
        summed = summed + factor * o
        weight = weight + factor * total
    out_ref[...] = (summed / weight).astype(out_ref.dtype)

    write = pltpu.make_async_copy(out_ref, out_hbm, out_sem)
    write.start()
    others = pl.ds(1, PEERS - 1)
    for buffer, rows, sem in ((msg_out, MSG, msg_send), (res_out, RES, res_send)):
        sent = buffer.at[others, pl.ds(0, rows)]
        pltpu.make_async_copy(sent, sent, sem).wait()
    write.wait()


def per_device(queries, request_of, selected, cache_keys, cache_values, recent_keys, recent_values):
    q = queries.reshape(ROWS, KVH * PER_KV, HD).transpose(1, 0, 2).reshape(128, HD)
    blocks = lambda a: a.reshape(PEERS, BLOCK, HD)
    recents = lambda a: a.reshape(ROWS * KVH, RECENT, HD)
    vmem = lambda shape, kind: pltpu.VMEM(shape, kind)
    dma = pltpu.SemaphoreType.DMA
    bf16, f32 = jnp.bfloat16, jnp.float32
    out = pl.pallas_call(
        kernel,
        out_shape=jax.ShapeDtypeStruct((32, HD), bf16),
        in_specs=[pl.BlockSpec(memory_space=pltpu.HBM)] * 7,
        out_specs=pl.BlockSpec(memory_space=pltpu.HBM),
        scratch_shapes=[
            pltpu.SMEM((ROWS, HEADS, TOP), jnp.int32),
            pltpu.SMEM((ROWS,), jnp.int32),
            vmem((32, HD), bf16),
            vmem((128, HD), bf16),
            vmem((PEERS, BLOCK, HD), bf16),
            vmem((PEERS, BLOCK, HD), bf16),
            vmem((ROWS * KVH, RECENT, HD), bf16),
            vmem((ROWS * KVH, RECENT, HD), bf16),
            vmem((128, HD), bf16),
            vmem((PEERS, 8, HD), bf16),
            vmem((PEERS, 8, HD), bf16),
            vmem((PEERS, 8, HD), f32),
            vmem((PEERS, 8, HD), f32),
            vmem((KVH, 2, 16, HD), f32),
            vmem((NG, HEADS, 2, 16, HD), f32),
            vmem((TOP, 32, HD), f32),
            vmem((TOP, 32, HD), f32),
            dma((7,)),
            dma,
            dma,
            dma((len(WAVES),)),
            dma,
            dma,
            dma((NG,)),
            dma((NG,)),
        ],
        compiler_params=pltpu.CompilerParams(
            collective_id=0, has_side_effects=True, vmem_limit_bytes=67043328
        ),
    )(
        selected, request_of, q, blocks(cache_keys), blocks(cache_values),
        recents(recent_keys), recents(recent_values),
    )
    return out.reshape(HEADS * PER_KV, ROWS, HD).transpose(1, 0, 2).reshape(ROWS, HEADS * PER_KV * HD)


def solution(mesh):
    return jax.shard_map(
        per_device,
        mesh=mesh,
        in_specs=(
            P("cache", None),
            P("cache"),
            P("cache", "group", None),
            P(None, "group", "cache", None),
            P(None, "group", "cache", None),
            P("cache", None, "group", None),
            P("cache", None, "group", None),
        ),
        out_specs=P("cache", "group"),
        check_vma=False,
    )
```

```python
import functools

import jax
import jax.numpy as jnp
from jax import lax
from jax.experimental import pallas as pl
from jax.experimental.pallas import tpu as pltpu
from jax.sharding import PartitionSpec as P

MESH = pl.DeviceIdType.MESH
NY, NZ, NC, NG = 4, 8, 2, 4
PEERS = NY * NZ * NC
ROWS, HEADS, PER_KV, TOP = 4, 2, 4, 4
KVH, HD, BLOCK = 8, 128, 128
RECENT = 256
SCALE = HD ** (-0.5)
MSG = 6
RES = 5
AHEAD = 2
WANTED = ROWS * HEADS * TOP


def signed(j):
    return ((j + 1) // 2) * (2 * (j % 2) - 1)


def hops(chip):
    return abs(signed(chip // NY)) + abs(signed(chip % NY))


CHIPS = sorted(range(NY * NZ), key=hops)
WAVES = [[chip for chip in CHIPS if hops(chip) in at] for at in ((0, 1), (2,), (3,), (4,), (5,), (6,))]
WAVE_OF = {chip: n for n, wave in enumerate(WAVES) for chip in wave}


def iota(shape, dim):
    return lax.broadcasted_iota(jnp.int32, shape, dim)


def high_low(p):
    high = p.astype(jnp.bfloat16)
    low = (p - high.astype(jnp.float32)).astype(jnp.bfloat16)
    return jnp.concatenate([high, low], axis=0)


def dot_t(a, b):
    return lax.dot_general(a, b, (((1,), (1,)), ((), ())), preferred_element_type=jnp.float32)


def dot(a, b):
    return jnp.dot(a, b, preferred_element_type=jnp.float32)


def kernel(
    sel_hbm, req_hbm, q_hbm, ck_ref, cv_ref, rk_ref, rv_ref, out_ref,
    sel_ref, req_ref, q_ref, ck, cv, rk, rv, rhs, msg_out, msg_in, res_out, res_in, near_out, near_in, far_o, far_s,
    load_sem, msg_send, msg_recv, res_send, res_recv, near_send, near_recv,
):
    cache = lax.axis_index("cache")
    group = lax.axis_index("group")
    y = lax.div(cache, NZ * NC)
    z = lax.rem(lax.div(cache, NC), NZ)
    c = lax.rem(cache, NC)
    other_z = [lax.rem(z + (NZ + signed(jz)), NZ) * NC for jz in range(NZ)]
    other_y = [lax.rem(y + (NY + signed(jy)), NY) * (NZ * NC) for jy in range(NY)]
    other_c = [c, 1 - c]
    other_yc = [other_y[i // NC] + other_c[i % NC] for i in range(NY * NC)]
    opposite = lambda j, n: 0 if j == 0 else (j + 1 if j % 2 and j + 1 < n else j if j % 2 else j - 1)

    def ahead(j):
        return (other_z[j // 8] + other_yc[j % 8], group)

    def behind(j):
        jz, jy, jc = opposite(j // 8, NZ), opposite(j // NC % NY, NY), j % NC
        return (other_z[jz] + other_yc[jy * NC + jc], group)

    barrier = pltpu.get_barrier_semaphore()
    order = [2 * chip + i for chip in reversed(CHIPS) for i in (1, 0) if chip + i]
    for j in order:
        pl.semaphore_signal(barrier, inc=1, device_id=ahead(j), device_id_type=MESH)
    for dg in range(1, NG):
        pl.semaphore_signal(
            barrier, inc=1, device_id=(cache, lax.rem(group + dg, NG)), device_id_type=MESH
        )

    loads = [
        pltpu.make_async_copy(src, dst, load_sem.at[i])
        for i, (src, dst) in enumerate(
            (
                (sel_hbm, sel_ref), (req_hbm, req_ref), (q_hbm, q_ref),
                (rk_ref, rk), (rv_ref, rv), (ck_ref, ck), (cv_ref, cv),
            )
        )
    ]
    for load in loads:
        load.start()

    loads[0].wait()
    loads[1].wait()

    lane = iota((8, 128), 1)
    wanted_by = [jnp.full((8, 128), -1, jnp.int32) for _ in range(TOP)]
    codes = jnp.zeros((WANTED, 128), jnp.int32)
    code_row = iota((WANTED, 128), 0)
    for r in range(ROWS):
        prompt = req_ref[r]
        for h in range(HEADS):
            here = (lane < 32) & (lane // 16 == h) & (lane % 4 == r)
            for k in range(TOP):
                e = (r * HEADS + h) * TOP + k
                block = sel_ref[r, h, k]
                owner = lax.shift_right_logical(block, 1)
                wanted_by[k] = jnp.where(here, owner, wanted_by[k])
                wanted_by[0] = jnp.where(lane == 32 + e, owner, wanted_by[0])
                code = prompt * 4 + h * 2 + (block - owner * 2) + 1
                codes = jnp.where(code_row == e, code, codes)
    wanted_by = [jnp.broadcast_to(w[0:1], (64, 128)) for w in wanted_by]
    loads[2].wait()
    rhs[0:32, :] = q_ref[pl.ds(pl.multiple_of(group * 32, 32), 32), :]
    rhs[32:64, :] = codes.astype(jnp.float32).astype(jnp.bfloat16)
    rhs[64:128, :] = jnp.zeros((64, 128), jnp.bfloat16)
    table = rhs[...]
    row64 = iota((64, 128), 0)
    lane64 = iota((64, 128), 1)
    half = row64 // 8 % 2
    place = row64 % 8
    col_row = jnp.where(lane64 < 32, lane64 // 4 % 4 + 4 * half, jnp.where(lane64 < 64, 4 - half, 9))
    row_match = place == col_row
    base = jnp.zeros((64, 128), jnp.int32)
    for i in range(8):
        base = jnp.where(row64 // 8 == i, other_yc[i], base)
    for jz in range(NZ):
        owner = base + other_z[jz]
        hit = wanted_by[0] == owner
        for k in range(1, TOP):
            hit = hit | (wanted_by[k] == owner)
        pick = jnp.where(hit & row_match, 1.0, 0.0).astype(jnp.bfloat16)
        msg_out[jz * 8 : (jz + 1) * 8] = dot(pick, table).reshape(8, 8, 128).astype(jnp.bfloat16)

    pl.semaphore_wait(barrier, PEERS - 1 + NG - 1)

    def message(j):
        at = pl.ds(0, MSG) if j % 2 == 0 else pl.ds(8 - MSG, MSG)
        return pltpu.make_async_remote_copy(
            src_ref=msg_out.at[j, at],
            dst_ref=msg_in.at[j, at],
            send_sem=msg_send,
            recv_sem=msg_recv.at[WAVE_OF[j // 2]],
            device_id=ahead(j),
            device_id_type=MESH,
        )

    for j in order:
        message(j).start()
    own_message = pltpu.make_async_copy(
        msg_out.at[0, pl.ds(0, MSG)], msg_in.at[0, pl.ds(0, MSG)], msg_recv.at[0]
    )
    own_message.start()

    loads[3].wait()
    loads[4].wait()
    row16 = iota((16, RECENT), 0) % ROWS
    row32 = iota((32, HD), 0) % ROWS
    lane16 = iota((16, HD), 1)

    def recent_scores(h):
        x = q_ref[h * 16 : (h + 1) * 16, :]
        s = dot_t(x, rk[h])
        for r in range(1, ROWS):
            s = jnp.where(row16 == r, dot_t(x, rk[r * KVH + h]), s)
        return s * SCALE

    def recent_rest(h, s):
        m = jnp.max(s, axis=1, keepdims=True)
        p = jnp.exp(s - m)
        total = jnp.sum(p, axis=1, keepdims=True)
        both = high_low(p)
        o = dot(both, rv[h])
        for r in range(1, ROWS):
            o = jnp.where(row32 == r, dot(both, rv[r * KVH + h]), o)
        near_out[h, 0] = o[0:16] + o[16:32]
        near_out[h, 1] = jnp.where(lane16 < 64, m, total)

    pending = []
    for h in range(KVH):
        pending.append((h, recent_scores(h)))
        if h >= AHEAD:
            recent_rest(*pending.pop(0))
    for item in pending:
        recent_rest(*item)

    nears = []
    for dg in range(1, NG):
        target = lax.rem(group + dg, NG)
        nears.append(
            pltpu.make_async_remote_copy(
                src_ref=near_out.at[pl.ds(target * HEADS, HEADS)],
                dst_ref=near_in.at[dg],
                send_sem=near_send.at[dg],
                recv_sem=near_recv.at[dg],
                device_id=(cache, target),
                device_id_type=MESH,
            )
        )
    for near in nears:
        near.start()

    loads[5].wait()
    loads[6].wait()

    def result(j):
        return pltpu.make_async_remote_copy(
            src_ref=res_out.at[j, pl.ds(0, RES)],
            dst_ref=res_in.at[cache, pl.ds(0, RES)],
            send_sem=res_send,
            recv_sem=res_recv,
            device_id=behind(j),
            device_id_type=MESH,
        )

    own_result = pltpu.make_async_copy(
        res_out.at[0, pl.ds(0, RES)], res_in.at[cache, pl.ds(0, RES)], res_recv
    )
    row8 = iota((8, 128), 0)
    upper = row8 < PER_KV
    m_first = upper & (lane == row8)
    t_first = upper & (lane == row8 + PER_KV)
    m_second = (~upper) & (lane == row8 - PER_KV)
    t_second = (~upper) & (lane == row8)

    def block_of(x, row):
        code = x[row : row + 1, :].astype(jnp.float32)[0, 0].astype(jnp.int32)
        return jnp.clip(code - 1, 0, PEERS - 1)

    def far(n):
        wave = WAVES[n]
        arrived = msg_in.at[pl.ds(0, 2 * len(wave)), pl.ds(0, MSG)]
        pltpu.make_async_copy(arrived, arrived, msg_recv.at[n]).wait()
        pairs = []
        for chip in wave:
            first, second = msg_in[2 * chip], msg_in[2 * chip + 1]
            a, b = block_of(first, 4), block_of(second, 3)
            x = jnp.where(upper, first.astype(jnp.float32), second.astype(jnp.float32))
            pairs.append((x.astype(jnp.bfloat16), a, b))
        scores = []
        for x, a, b in pairs:
            s = dot_t(x, jnp.concatenate([ck[a], ck[b]], axis=0))
            scores.append(jnp.where(upper, s[:, :BLOCK], s[:, BLOCK:]) * SCALE)
        highs = [jnp.max(s, axis=1, keepdims=True) for s in scores]
        weights = [jnp.exp(s - m) for s, m in zip(scores, highs)]
        totals = [jnp.sum(p, axis=1, keepdims=True) for p in weights]
        for chip, (x, a, b), p, m, t in zip(wave, pairs, weights, highs, totals):
            both = high_low(
                jnp.concatenate([jnp.where(upper, p, 0.0), jnp.where(upper, 0.0, p)], axis=1)
            )
            o = dot(both, jnp.concatenate([cv[a], cv[b]], axis=0))
            o = o[0:8] + o[8:16]
            one = jnp.sum(jnp.where(m_first, m, jnp.where(t_first, t, 0.0)), axis=0, keepdims=True)
            two = jnp.sum(jnp.where(m_second, m, jnp.where(t_second, t, 0.0)), axis=0, keepdims=True)
            res_out[2 * chip] = jnp.where(upper, o, one)
            res_out[2 * chip + 1] = jnp.where(upper, pltpu.roll(o, PER_KV, 0), two)
        for chip in reversed(wave):
            for i in (1, 0):
                if chip + i:
                    result(2 * chip + i).start()
                else:
                    own_result.start()

    for n in range(len(WAVES)):
        far(n)

    for near in nears:
        near.wait()

    def merged(parts):
        peak = functools.reduce(jnp.maximum, [m for _, m, _ in parts])
        summed, weight = 0.0, 0.0
        for o, m, total in parts:
            factor = jnp.exp(m - peak)
            summed = summed + factor * o
            weight = weight + factor * total
        return summed, peak, weight

    parts = []
    for dg in range(NG):
        if dg:
            both = near_in[dg]
        else:
            both = near_out[pl.ds(group * HEADS, HEADS)]
        stat = both[:, 1].reshape(32, 128)
        parts.append((both[:, 0].reshape(32, 128), stat[:, 0:1], stat[:, 64:65]))
    parts = [merged(parts)]

    returned = pl.ds(0, RES)
    pltpu.make_async_copy(res_out.at[:, returned], res_in.at[:, returned], res_recv).wait()

    for r in range(ROWS):
        for h in range(HEADS):
            for k in range(TOP):
                tile = res_in[lax.shift_right_logical(sel_ref[r, h, k], 1)]
                rows = pl.ds(h * 16 + r, 4, stride=4)
                far_o[k, rows, :] = tile[0:4]
                far_s[k, rows, :] = jnp.broadcast_to(tile[4:5], (4, 128))
    lane32 = iota((32, 128), 1)
    which = iota((32, 128), 0) // 4 % 4
    for k in range(TOP):
        stat = far_s[k]
        m = jnp.sum(jnp.where(lane32 == which, stat, 0.0), axis=1, keepdims=True)
        total = jnp.sum(jnp.where(lane32 == which + PER_KV, stat, 0.0), axis=1, keepdims=True)
        parts.append((far_o[k], m, total))
    summed, _, weight = merged(parts)
    out_ref[...] = (summed / weight).astype(out_ref.dtype)

    others = pl.ds(1, PEERS - 1)
    for buffer, rows, sem in ((msg_out, MSG, msg_send), (res_out, RES, res_send)):
        sent = buffer.at[others, pl.ds(0, rows)]
        pltpu.make_async_copy(sent, sent, sem).wait()


def per_device(queries, request_of, selected, cache_keys, cache_values, recent_keys, recent_values):
    q = queries.reshape(ROWS, KVH * PER_KV, HD).transpose(1, 0, 2).reshape(128, HD)
    blocks = lambda a: a.reshape(PEERS, BLOCK, HD)
    recents = lambda a: a.reshape(ROWS * KVH, RECENT, HD)
    vmem = lambda shape, kind: pltpu.VMEM(shape, kind)
    dma = pltpu.SemaphoreType.DMA
    bf16, f32 = jnp.bfloat16, jnp.float32
    out = pl.pallas_call(
        kernel,
        out_shape=jax.ShapeDtypeStruct((32, HD), bf16),
        in_specs=[pl.BlockSpec(memory_space=pltpu.HBM)] * 7,
        out_specs=pl.BlockSpec(memory_space=pltpu.VMEM),
        scratch_shapes=[
            pltpu.SMEM((ROWS, HEADS, TOP), jnp.int32),
            pltpu.SMEM((ROWS,), jnp.int32),
            vmem((128, HD), bf16),
            vmem((PEERS, BLOCK, HD), bf16),
            vmem((PEERS, BLOCK, HD), bf16),
            vmem((ROWS * KVH, RECENT, HD), bf16),
            vmem((ROWS * KVH, RECENT, HD), bf16),
            vmem((128, HD), bf16),
            vmem((PEERS, 8, HD), bf16),
            vmem((PEERS, 8, HD), bf16),
            vmem((PEERS, 8, HD), f32),
            vmem((PEERS, 8, HD), f32),
            vmem((KVH, 2, 16, HD), f32),
            vmem((NG, HEADS, 2, 16, HD), f32),
            vmem((TOP, 32, HD), f32),
            vmem((TOP, 32, HD), f32),
            dma((7,)),
            dma,
            dma((len(WAVES),)),
            dma,
            dma,
            dma((NG,)),
            dma((NG,)),
        ],
        compiler_params=pltpu.CompilerParams(
            collective_id=0, has_side_effects=True, vmem_limit_bytes=40 * 1024 * 1024
        ),
    )(
        *[
            pltpu.with_memory_space_constraint(a, pltpu.HBM)
            for a in (
                selected, request_of, q, blocks(cache_keys), blocks(cache_values),
                recents(recent_keys), recents(recent_values),
            )
        ]
    )
    return out.reshape(HEADS * PER_KV, ROWS, HD).transpose(1, 0, 2).reshape(ROWS, HEADS * PER_KV * HD)


def solution(mesh):
    return jax.shard_map(
        per_device,
        mesh=mesh,
        in_specs=(
            P("cache", None),
            P("cache"),
            P("cache", "group", None),
            P(None, "group", "cache", None),
            P(None, "group", "cache", None),
            P("cache", None, "group", None),
            P("cache", None, "group", None),
        ),
        out_specs=P("cache", "group"),
        check_vma=False,
    )
```

```python
import functools

import jax
import jax.numpy as jnp
from jax import lax
from jax.experimental import pallas as pl
from jax.experimental.pallas import tpu as pltpu
from jax.sharding import PartitionSpec as P

MESH = pl.DeviceIdType.MESH
NY, NZ, NC, NG = 4, 8, 2, 4
PEERS = NY * NZ * NC
ROWS, HEADS, PER_KV, TOP = 4, 2, 4, 4
KVH, HD, BLOCK = 8, 128, 128
RECENT = 256
SCALE = HD ** (-0.5)
MSG = 6
RES = 5
AHEAD = 2
URGENT = 4
WANTED = ROWS * HEADS * TOP


def signed(j):
    return ((j + 1) // 2) * (2 * (j % 2) - 1)


def hops(chip):
    return abs(signed(chip // NY)) + abs(signed(chip % NY))


CHIPS = sorted(range(NY * NZ), key=hops)
WAVES = [[chip for chip in CHIPS if hops(chip) in at] for at in ((0, 1), (2,), (3,), (4,), (5,), (6,))]
WAVE_OF = {chip: n for n, wave in enumerate(WAVES) for chip in wave}


def iota(shape, dim):
    return lax.broadcasted_iota(jnp.int32, shape, dim)


def high_low(p):
    high = p.astype(jnp.bfloat16)
    low = (p - high.astype(jnp.float32)).astype(jnp.bfloat16)
    return jnp.concatenate([high, low], axis=0)


def dot_t(a, b):
    return lax.dot_general(a, b, (((1,), (1,)), ((), ())), preferred_element_type=jnp.float32)


def dot(a, b):
    return jnp.dot(a, b, preferred_element_type=jnp.float32)


def kernel(
    sel_hbm, req_hbm, q_hbm, ck_ref, cv_ref, rk_ref, rv_ref, out_ref,
    sel_ref, req_ref, q_ref, ck, cv, rk, rv, rhs, msg_out, msg_in, res_out, res_in, near_out, near_in, far_o, far_s,
    load_sem, msg_send, msg_recv, res_send, res_recv, near_send, near_recv,
):
    cache = lax.axis_index("cache")
    group = lax.axis_index("group")
    y = lax.div(cache, NZ * NC)
    z = lax.rem(lax.div(cache, NC), NZ)
    c = lax.rem(cache, NC)
    other_z = [lax.rem(z + (NZ + signed(jz)), NZ) * NC for jz in range(NZ)]
    other_y = [lax.rem(y + (NY + signed(jy)), NY) * (NZ * NC) for jy in range(NY)]
    other_c = [c, 1 - c]
    other_yc = [other_y[i // NC] + other_c[i % NC] for i in range(NY * NC)]
    opposite = lambda j, n: 0 if j == 0 else (j + 1 if j % 2 and j + 1 < n else j if j % 2 else j - 1)

    def ahead(j):
        return (other_z[j // 8] + other_yc[j % 8], group)

    def behind(j):
        jz, jy, jc = opposite(j // 8, NZ), opposite(j // NC % NY, NY), j % NC
        return (other_z[jz] + other_yc[jy * NC + jc], group)

    barrier = pltpu.get_barrier_semaphore()
    order = [2 * chip + i for chip in reversed(CHIPS) for i in (1, 0) if chip + i]
    for j in order:
        pl.semaphore_signal(barrier, inc=1, device_id=ahead(j), device_id_type=MESH)
    for dg in range(1, NG):
        pl.semaphore_signal(
            barrier, inc=1, device_id=(cache, lax.rem(group + dg, NG)), device_id_type=MESH
        )

    loads = [
        pltpu.make_async_copy(src, dst, load_sem.at[i])
        for i, (src, dst) in enumerate(
            (
                (sel_hbm, sel_ref), (req_hbm, req_ref), (q_hbm, q_ref),
                (rk_ref, rk), (rv_ref, rv), (ck_ref, ck), (cv_ref, cv),
            )
        )
    ]
    for load in loads:
        load.start()

    loads[0].wait()
    loads[1].wait()

    lane = iota((8, 128), 1)
    wanted_by = [jnp.full((8, 128), -1, jnp.int32) for _ in range(TOP)]
    codes = jnp.zeros((WANTED, 128), jnp.int32)
    code_row = iota((WANTED, 128), 0)
    for r in range(ROWS):
        prompt = req_ref[r]
        for h in range(HEADS):
            here = (lane < 32) & (lane // 16 == h) & (lane % 4 == r)
            for k in range(TOP):
                e = (r * HEADS + h) * TOP + k
                block = sel_ref[r, h, k]
                owner = lax.shift_right_logical(block, 1)
                wanted_by[k] = jnp.where(here, owner, wanted_by[k])
                wanted_by[0] = jnp.where(lane == 32 + e, owner, wanted_by[0])
                code = prompt * 4 + h * 2 + (block - owner * 2) + 1
                codes = jnp.where(code_row == e, code, codes)
    wanted_by = [jnp.broadcast_to(w[0:1], (64, 128)) for w in wanted_by]
    loads[2].wait()
    rhs[0:32, :] = q_ref[pl.ds(pl.multiple_of(group * 32, 32), 32), :]
    rhs[32:64, :] = codes.astype(jnp.float32).astype(jnp.bfloat16)
    rhs[64:128, :] = jnp.zeros((64, 128), jnp.bfloat16)
    table = rhs[...]
    row64 = iota((64, 128), 0)
    lane64 = iota((64, 128), 1)
    half = row64 // 8 % 2
    place = row64 % 8
    col_row = jnp.where(lane64 < 32, lane64 // 4 % 4 + 4 * half, jnp.where(lane64 < 64, 4 - half, 9))
    row_match = place == col_row
    base = jnp.zeros((64, 128), jnp.int32)
    for i in range(8):
        base = jnp.where(row64 // 8 == i, other_yc[i], base)
    for jz in range(NZ):
        owner = base + other_z[jz]
        hit = wanted_by[0] == owner
        for k in range(1, TOP):
            hit = hit | (wanted_by[k] == owner)
        pick = jnp.where(hit & row_match, 1.0, 0.0).astype(jnp.bfloat16)
        msg_out[jz * 8 : (jz + 1) * 8] = dot(pick, table).reshape(8, 8, 128).astype(jnp.bfloat16)

    pl.semaphore_wait(barrier, PEERS - 1 + NG - 1)

    def message(j):
        at = pl.ds(0, MSG) if j % 2 == 0 else pl.ds(8 - MSG, MSG)
        return pltpu.make_async_remote_copy(
            src_ref=msg_out.at[j, at],
            dst_ref=msg_in.at[j, at],
            send_sem=msg_send,
            recv_sem=msg_recv.at[WAVE_OF[j // 2]],
            device_id=ahead(j),
            device_id_type=MESH,
        )

    for j in order:
        message(j).start()
    own_message = pltpu.make_async_copy(
        msg_out.at[0, pl.ds(0, MSG)], msg_in.at[0, pl.ds(0, MSG)], msg_recv.at[0]
    )
    own_message.start()

    loads[3].wait()
    loads[4].wait()
    row16 = iota((16, RECENT), 0) % ROWS
    row32 = iota((32, HD), 0) % ROWS
    lane16 = iota((16, HD), 1)

    def recent_scores(h):
        x = q_ref[h * 16 : (h + 1) * 16, :]
        s = dot_t(x, rk[h])
        for r in range(1, ROWS):
            s = jnp.where(row16 == r, dot_t(x, rk[r * KVH + h]), s)
        return s * SCALE

    def recent_rest(h, s):
        m = jnp.max(s, axis=1, keepdims=True)
        p = jnp.exp(s - m)
        total = jnp.sum(p, axis=1, keepdims=True)
        both = high_low(p)
        o = dot(both, rv[h])
        for r in range(1, ROWS):
            o = jnp.where(row32 == r, dot(both, rv[r * KVH + h]), o)
        near_out[h, 0] = o[0:16] + o[16:32]
        near_out[h, 1] = jnp.where(lane16 < 64, m, total)

    pending = []
    for h in range(KVH):
        pending.append((h, recent_scores(h)))
        if h >= AHEAD:
            recent_rest(*pending.pop(0))
    for item in pending:
        recent_rest(*item)

    nears = []
    for dg in range(1, NG):
        target = lax.rem(group + dg, NG)
        nears.append(
            pltpu.make_async_remote_copy(
                src_ref=near_out.at[pl.ds(target * HEADS, HEADS)],
                dst_ref=near_in.at[dg],
                send_sem=near_send.at[dg],
                recv_sem=near_recv.at[dg],
                device_id=(cache, target),
                device_id_type=MESH,
            )
        )
    for near in nears:
        near.start()

    loads[5].wait()
    loads[6].wait()

    def result(j):
        return pltpu.make_async_remote_copy(
            src_ref=res_out.at[j, pl.ds(0, RES)],
            dst_ref=res_in.at[cache, pl.ds(0, RES)],
            send_sem=res_send,
            recv_sem=res_recv,
            device_id=behind(j),
            device_id_type=MESH,
        )

    own_result = pltpu.make_async_copy(
        res_out.at[0, pl.ds(0, RES)], res_in.at[cache, pl.ds(0, RES)], res_recv
    )
    row8 = iota((8, 128), 0)
    upper = row8 < PER_KV
    m_first = upper & (lane == row8)
    t_first = upper & (lane == row8 + PER_KV)
    m_second = (~upper) & (lane == row8 - PER_KV)
    t_second = (~upper) & (lane == row8)

    def block_of(x, row):
        code = x[row : row + 1, :].astype(jnp.float32)[0, 0].astype(jnp.int32)
        return jnp.clip(code - 1, 0, PEERS - 1)

    def urgent(jz):
        return other_z[opposite(jz, NZ)] < URGENT * NC

    def send_back(chips):
        for chip in reversed(chips):
            for i in (1, 0):
                if chip + i:
                    result(2 * chip + i).start()
                else:
                    own_result.start()

    def far(n):
        wave = WAVES[n]
        arrived = msg_in.at[pl.ds(0, 2 * len(wave)), pl.ds(0, MSG)]
        pltpu.make_async_copy(arrived, arrived, msg_recv.at[n]).wait()
        pairs = []
        for chip in wave:
            first, second = msg_in[2 * chip], msg_in[2 * chip + 1]
            a, b = block_of(first, 4), block_of(second, 3)
            x = jnp.where(upper, first.astype(jnp.float32), second.astype(jnp.float32))
            pairs.append((x.astype(jnp.bfloat16), a, b))
        scores = []
        for x, a, b in pairs:
            s = dot_t(x, jnp.concatenate([ck[a], ck[b]], axis=0))
            scores.append(jnp.where(upper, s[:, :BLOCK], s[:, BLOCK:]) * SCALE)
        highs = [jnp.max(s, axis=1, keepdims=True) for s in scores]
        weights = [jnp.exp(s - m) for s, m in zip(scores, highs)]
        totals = [jnp.sum(p, axis=1, keepdims=True) for p in weights]
        for chip, (x, a, b), p, m, t in zip(wave, pairs, weights, highs, totals):
            both = high_low(
                jnp.concatenate([jnp.where(upper, p, 0.0), jnp.where(upper, 0.0, p)], axis=1)
            )
            o = dot(both, jnp.concatenate([cv[a], cv[b]], axis=0))
            o = o[0:8] + o[8:16]
            one = jnp.sum(jnp.where(m_first, m, jnp.where(t_first, t, 0.0)), axis=0, keepdims=True)
            two = jnp.sum(jnp.where(m_second, m, jnp.where(t_second, t, 0.0)), axis=0, keepdims=True)
            res_out[2 * chip] = jnp.where(upper, o, one)
            res_out[2 * chip + 1] = jnp.where(upper, pltpu.roll(o, PER_KV, 0), two)
        for jz in range(NZ):
            chips = [chip for chip in wave if chip // NY == jz]
            if chips:
                pl.when(urgent(jz))(lambda: send_back(chips))

    for n in range(len(WAVES)):
        far(n)
    for jz in reversed(range(NZ)):
        chips = [chip for chip in CHIPS if chip // NY == jz]
        pl.when(jnp.logical_not(urgent(jz)))(lambda: send_back(chips))

    for near in nears:
        near.wait()

    def merged(parts):
        peak = functools.reduce(jnp.maximum, [m for _, m, _ in parts])
        summed, weight = 0.0, 0.0
        for o, m, total in parts:
            factor = jnp.exp(m - peak)
            summed = summed + factor * o
            weight = weight + factor * total
        return summed, peak, weight

    parts = []
    for dg in range(NG):
        if dg:
            both = near_in[dg]
        else:
            both = near_out[pl.ds(group * HEADS, HEADS)]
        stat = both[:, 1].reshape(32, 128)
        parts.append((both[:, 0].reshape(32, 128), stat[:, 0:1], stat[:, 64:65]))
    parts = [merged(parts)]

    returned = pl.ds(0, RES)
    pltpu.make_async_copy(res_out.at[:, returned], res_in.at[:, returned], res_recv).wait()

    for r in range(ROWS):
        for h in range(HEADS):
            for k in range(TOP):
                tile = res_in[lax.shift_right_logical(sel_ref[r, h, k], 1)]
                rows = pl.ds(h * 16 + r, 4, stride=4)
                far_o[k, rows, :] = tile[0:4]
                far_s[k, rows, :] = jnp.broadcast_to(tile[4:5], (4, 128))
    lane32 = iota((32, 128), 1)
    which = iota((32, 128), 0) // 4 % 4
    for k in range(TOP):
        stat = far_s[k]
        m = jnp.sum(jnp.where(lane32 == which, stat, 0.0), axis=1, keepdims=True)
        total = jnp.sum(jnp.where(lane32 == which + PER_KV, stat, 0.0), axis=1, keepdims=True)
        parts.append((far_o[k], m, total))
    summed, _, weight = merged(parts)
    out_ref[...] = (summed / weight).astype(out_ref.dtype)

    others = pl.ds(1, PEERS - 1)
    for buffer, rows, sem in ((msg_out, MSG, msg_send), (res_out, RES, res_send)):
        sent = buffer.at[others, pl.ds(0, rows)]
        pltpu.make_async_copy(sent, sent, sem).wait()


def per_device(queries, request_of, selected, cache_keys, cache_values, recent_keys, recent_values):
    q = queries.reshape(ROWS, KVH * PER_KV, HD).transpose(1, 0, 2).reshape(128, HD)
    blocks = lambda a: a.reshape(PEERS, BLOCK, HD)
    recents = lambda a: a.reshape(ROWS * KVH, RECENT, HD)
    vmem = lambda shape, kind: pltpu.VMEM(shape, kind)
    dma = pltpu.SemaphoreType.DMA
    bf16, f32 = jnp.bfloat16, jnp.float32
    out = pl.pallas_call(
        kernel,
        out_shape=jax.ShapeDtypeStruct((32, HD), bf16),
        in_specs=[pl.BlockSpec(memory_space=pltpu.HBM)] * 7,
        out_specs=pl.BlockSpec(memory_space=pltpu.VMEM),
        scratch_shapes=[
            pltpu.SMEM((ROWS, HEADS, TOP), jnp.int32),
            pltpu.SMEM((ROWS,), jnp.int32),
            vmem((128, HD), bf16),
            vmem((PEERS, BLOCK, HD), bf16),
            vmem((PEERS, BLOCK, HD), bf16),
            vmem((ROWS * KVH, RECENT, HD), bf16),
            vmem((ROWS * KVH, RECENT, HD), bf16),
            vmem((128, HD), bf16),
            vmem((PEERS, 8, HD), bf16),
            vmem((PEERS, 8, HD), bf16),
            vmem((PEERS, 8, HD), f32),
            vmem((PEERS, 8, HD), f32),
            vmem((KVH, 2, 16, HD), f32),
            vmem((NG, HEADS, 2, 16, HD), f32),
            vmem((TOP, 32, HD), f32),
            vmem((TOP, 32, HD), f32),
            dma((7,)),
            dma,
            dma((len(WAVES),)),
            dma,
            dma,
            dma((NG,)),
            dma((NG,)),
        ],
        compiler_params=pltpu.CompilerParams(
            collective_id=0, has_side_effects=True, vmem_limit_bytes=40 * 1024 * 1024
        ),
    )(
        *[
            pltpu.with_memory_space_constraint(a, pltpu.HBM)
            for a in (
                selected, request_of, q, blocks(cache_keys), blocks(cache_values),
                recents(recent_keys), recents(recent_values),
            )
        ]
    )
    return out.reshape(HEADS * PER_KV, ROWS, HD).transpose(1, 0, 2).reshape(ROWS, HEADS * PER_KV * HD)


def solution(mesh):
    return jax.shard_map(
        per_device,
        mesh=mesh,
        in_specs=(
            P("cache", None),
            P("cache"),
            P("cache", "group", None),
            P(None, "group", "cache", None),
            P(None, "group", "cache", None),
            P("cache", None, "group", None),
            P("cache", None, "group", None),
        ),
        out_specs=P("cache", "group"),
        check_vma=False,
    )
```

```python
import functools

import jax
import jax.numpy as jnp
from jax import lax
from jax.experimental import pallas as pl
from jax.experimental.pallas import tpu as pltpu
from jax.sharding import PartitionSpec as P

MESH = pl.DeviceIdType.MESH
NY, NZ, NC, NG = 4, 8, 2, 4
PEERS = NY * NZ * NC
ROWS, HEADS, PER_KV, TOP = 4, 2, 4, 4
KVH, HD, BLOCK = 8, 128, 128
RECENT = 256
SCALE = HD ** (-0.5)
MSG = 6
RES = 5
AHEAD = 2
URGENT = 4
WANTED = ROWS * HEADS * TOP


def signed(j):
    return ((j + 1) // 2) * (2 * (j % 2) - 1)


def hops(chip):
    return abs(signed(chip // NY)) + abs(signed(chip % NY))


CHIPS = sorted(range(NY * NZ), key=hops)
WAVES = [[chip for chip in CHIPS if hops(chip) in at] for at in ((0, 1), (2,), (3,), (4,), (5,), (6,))]
WAVE_OF = {chip: n for n, wave in enumerate(WAVES) for chip in wave}


def iota(shape, dim):
    return lax.broadcasted_iota(jnp.int32, shape, dim)


def high_low(p):
    high = p.astype(jnp.bfloat16)
    low = (p - high.astype(jnp.float32)).astype(jnp.bfloat16)
    return jnp.concatenate([high, low], axis=0)


def dot_t(a, b):
    return lax.dot_general(a, b, (((1,), (1,)), ((), ())), preferred_element_type=jnp.float32)


def dot(a, b):
    return jnp.dot(a, b, preferred_element_type=jnp.float32)


def kernel(
    sel_hbm, req_hbm, q_hbm, ck_ref, cv_ref, rk_ref, rv_ref, out_ref,
    sel_ref, req_ref, q_ref, ck, cv, rk, rv, rhs, msg_out, msg_in, res_out, res_in, near_out, near_in, far_o, far_s,
    load_sem, msg_send, msg_recv, res_send, res_recv, near_send, near_recv,
):
    cache = lax.axis_index("cache")
    group = lax.axis_index("group")
    y = lax.div(cache, NZ * NC)
    z = lax.rem(lax.div(cache, NC), NZ)
    c = lax.rem(cache, NC)
    other_z = [lax.rem(z + (NZ + signed(jz)), NZ) * NC for jz in range(NZ)]
    other_y = [lax.rem(y + (NY + signed(jy)), NY) * (NZ * NC) for jy in range(NY)]
    other_c = [c, 1 - c]
    other_yc = [other_y[i // NC] + other_c[i % NC] for i in range(NY * NC)]
    opposite = lambda j, n: 0 if j == 0 else (j + 1 if j % 2 and j + 1 < n else j if j % 2 else j - 1)

    def ahead(j):
        return (other_z[j // 8] + other_yc[j % 8], group)

    def behind(j):
        jz, jy, jc = opposite(j // 8, NZ), opposite(j // NC % NY, NY), j % NC
        return (other_z[jz] + other_yc[jy * NC + jc], group)

    barrier = pltpu.get_barrier_semaphore()
    order = [2 * chip + i for chip in reversed(CHIPS) for i in (1, 0) if chip + i]
    for j in order:
        pl.semaphore_signal(barrier, inc=1, device_id=ahead(j), device_id_type=MESH)
    for dg in range(1, NG):
        pl.semaphore_signal(
            barrier, inc=1, device_id=(cache, lax.rem(group + dg, NG)), device_id_type=MESH
        )

    loads = [
        pltpu.make_async_copy(src, dst, load_sem.at[i])
        for i, (src, dst) in enumerate(
            (
                (sel_hbm, sel_ref), (req_hbm, req_ref), (q_hbm, q_ref),
                (rk_ref, rk), (rv_ref, rv), (ck_ref, ck), (cv_ref, cv),
            )
        )
    ]
    for load in loads:
        load.start()

    loads[0].wait()
    loads[1].wait()

    lane = iota((8, 128), 1)
    wanted_by = [jnp.full((8, 128), -1, jnp.int32) for _ in range(TOP)]
    codes = jnp.zeros((WANTED, 128), jnp.int32)
    code_row = iota((WANTED, 128), 0)
    for r in range(ROWS):
        prompt = req_ref[r]
        for h in range(HEADS):
            here = (lane < 32) & (lane // 16 == h) & (lane % 4 == r)
            for k in range(TOP):
                e = (r * HEADS + h) * TOP + k
                block = sel_ref[r, h, k]
                owner = lax.shift_right_logical(block, 1)
                wanted_by[k] = jnp.where(here, owner, wanted_by[k])
                wanted_by[0] = jnp.where(lane == 32 + e, owner, wanted_by[0])
                code = prompt * 4 + h * 2 + (block - owner * 2) + 1
                codes = jnp.where(code_row == e, code, codes)
    wanted_by = [jnp.broadcast_to(w[0:1], (64, 128)) for w in wanted_by]
    loads[2].wait()
    rhs[0:32, :] = q_ref[pl.ds(pl.multiple_of(group * 32, 32), 32), :]
    rhs[32:64, :] = codes.astype(jnp.float32).astype(jnp.bfloat16)
    rhs[64:128, :] = jnp.zeros((64, 128), jnp.bfloat16)
    table = rhs[...]
    row64 = iota((64, 128), 0)
    lane64 = iota((64, 128), 1)
    half = row64 // 8 % 2
    place = row64 % 8
    col_row = jnp.where(lane64 < 32, lane64 // 4 % 4 + 4 * half, jnp.where(lane64 < 64, 4 - half, 9))
    row_match = place == col_row
    base = jnp.zeros((64, 128), jnp.int32)
    for i in range(8):
        base = jnp.where(row64 // 8 == i, other_yc[i], base)
    for jz in range(NZ):
        owner = base + other_z[jz]
        hit = wanted_by[0] == owner
        for k in range(1, TOP):
            hit = hit | (wanted_by[k] == owner)
        pick = jnp.where(hit & row_match, 1.0, 0.0).astype(jnp.bfloat16)
        msg_out[jz * 8 : (jz + 1) * 8] = dot(pick, table).reshape(8, 8, 128).astype(jnp.bfloat16)

    loads[3].wait()
    loads[4].wait()
    row16 = iota((16, RECENT), 0) % ROWS
    row32 = iota((32, HD), 0) % ROWS
    lane16 = iota((16, HD), 1)

    def recent_scores(h):
        x = q_ref[h * 16 : (h + 1) * 16, :]
        s = dot_t(x, rk[h])
        for r in range(1, ROWS):
            s = jnp.where(row16 == r, dot_t(x, rk[r * KVH + h]), s)
        return s * SCALE

    def recent_rest(h, s):
        m = jnp.max(s, axis=1, keepdims=True)
        p = jnp.exp(s - m)
        total = jnp.sum(p, axis=1, keepdims=True)
        both = high_low(p)
        o = dot(both, rv[h])
        for r in range(1, ROWS):
            o = jnp.where(row32 == r, dot(both, rv[r * KVH + h]), o)
        near_out[h, 0] = o[0:16] + o[16:32]
        near_out[h, 1] = jnp.where(lane16 < 64, m, total)

    pending = []
    for h in range(KVH):
        pending.append((h, recent_scores(h)))
        if h >= AHEAD:
            recent_rest(*pending.pop(0))
    for item in pending:
        recent_rest(*item)

    pl.semaphore_wait(barrier, PEERS - 1 + NG - 1)

    def message(j):
        at = pl.ds(0, MSG) if j % 2 == 0 else pl.ds(8 - MSG, MSG)
        return pltpu.make_async_remote_copy(
            src_ref=msg_out.at[j, at],
            dst_ref=msg_in.at[j, at],
            send_sem=msg_send,
            recv_sem=msg_recv.at[WAVE_OF[j // 2]],
            device_id=ahead(j),
            device_id_type=MESH,
        )

    for j in order[:10] + order[:9:-1]:
        message(j).start()
    own_message = pltpu.make_async_copy(
        msg_out.at[0, pl.ds(0, MSG)], msg_in.at[0, pl.ds(0, MSG)], msg_recv.at[0]
    )
    own_message.start()

    nears = []
    for dg in range(1, NG):
        target = lax.rem(group + dg, NG)
        nears.append(
            pltpu.make_async_remote_copy(
                src_ref=near_out.at[pl.ds(target * HEADS, HEADS)],
                dst_ref=near_in.at[dg],
                send_sem=near_send.at[dg],
                recv_sem=near_recv.at[dg],
                device_id=(cache, target),
                device_id_type=MESH,
            )
        )
    for near in nears:
        near.start()

    loads[5].wait()
    loads[6].wait()

    def result(j):
        return pltpu.make_async_remote_copy(
            src_ref=res_out.at[j, pl.ds(0, RES)],
            dst_ref=res_in.at[cache, pl.ds(0, RES)],
            send_sem=res_send,
            recv_sem=res_recv,
            device_id=behind(j),
            device_id_type=MESH,
        )

    own_result = pltpu.make_async_copy(
        res_out.at[0, pl.ds(0, RES)], res_in.at[cache, pl.ds(0, RES)], res_recv
    )
    row8 = iota((8, 128), 0)
    upper = row8 < PER_KV
    m_first = upper & (lane == row8)
    t_first = upper & (lane == row8 + PER_KV)
    m_second = (~upper) & (lane == row8 - PER_KV)
    t_second = (~upper) & (lane == row8)

    def block_of(x, row):
        code = x[row : row + 1, :].astype(jnp.float32)[0, 0].astype(jnp.int32)
        return jnp.clip(code - 1, 0, PEERS - 1)

    def urgent(jz):
        return other_z[opposite(jz, NZ)] < URGENT * NC

    def send_back(chips):
        for chip in reversed(chips):
            for i in (1, 0):
                if chip + i:
                    result(2 * chip + i).start()
                else:
                    own_result.start()

    def far(n):
        wave = WAVES[n]
        arrived = msg_in.at[pl.ds(0, 2 * len(wave)), pl.ds(0, MSG)]
        pltpu.make_async_copy(arrived, arrived, msg_recv.at[n]).wait()
        pairs = []
        for chip in wave:
            first, second = msg_in[2 * chip], msg_in[2 * chip + 1]
            a, b = block_of(first, 4), block_of(second, 3)
            x = jnp.where(upper, first.astype(jnp.float32), second.astype(jnp.float32))
            pairs.append((x.astype(jnp.bfloat16), a, b))
        scores = []
        for x, a, b in pairs:
            s = dot_t(x, jnp.concatenate([ck[a], ck[b]], axis=0))
            scores.append(jnp.where(upper, s[:, :BLOCK], s[:, BLOCK:]) * SCALE)
        highs = [jnp.max(s, axis=1, keepdims=True) for s in scores]
        weights = [jnp.exp(s - m) for s, m in zip(scores, highs)]
        totals = [jnp.sum(p, axis=1, keepdims=True) for p in weights]
        for chip, (x, a, b), p, m, t in zip(wave, pairs, weights, highs, totals):
            both = high_low(
                jnp.concatenate([jnp.where(upper, p, 0.0), jnp.where(upper, 0.0, p)], axis=1)
            )
            o = dot(both, jnp.concatenate([cv[a], cv[b]], axis=0))
            o = o[0:8] + o[8:16]
            one = jnp.sum(jnp.where(m_first, m, jnp.where(t_first, t, 0.0)), axis=0, keepdims=True)
            two = jnp.sum(jnp.where(m_second, m, jnp.where(t_second, t, 0.0)), axis=0, keepdims=True)
            res_out[2 * chip] = jnp.where(upper, o, one)
            res_out[2 * chip + 1] = jnp.where(upper, pltpu.roll(o, PER_KV, 0), two)
        for jz in range(NZ):
            chips = [chip for chip in wave if chip // NY == jz]
            if chips:
                pl.when(urgent(jz))(lambda: send_back(chips))

    for n in range(len(WAVES)):
        far(n)
    for jz in reversed(range(NZ)):
        chips = [chip for chip in CHIPS if chip // NY == jz]
        pl.when(jnp.logical_not(urgent(jz)))(lambda: send_back(chips))

    for near in nears:
        near.wait()

    def merged(parts):
        peak = functools.reduce(jnp.maximum, [m for _, m, _ in parts])
        summed, weight = 0.0, 0.0
        for o, m, total in parts:
            factor = jnp.exp(m - peak)
            summed = summed + factor * o
            weight = weight + factor * total
        return summed, peak, weight

    parts = []
    for dg in range(NG):
        if dg:
            both = near_in[dg]
        else:
            both = near_out[pl.ds(group * HEADS, HEADS)]
        stat = both[:, 1].reshape(32, 128)
        parts.append((both[:, 0].reshape(32, 128), stat[:, 0:1], stat[:, 64:65]))
    parts = [merged(parts)]

    returned = pl.ds(0, RES)
    pltpu.make_async_copy(res_out.at[:, returned], res_in.at[:, returned], res_recv).wait()

    for r in range(ROWS):
        for h in range(HEADS):
            for k in range(TOP):
                tile = res_in[lax.shift_right_logical(sel_ref[r, h, k], 1)]
                rows = pl.ds(h * 16 + r, 4, stride=4)
                far_o[k, rows, :] = tile[0:4]
                far_s[k, rows, :] = jnp.broadcast_to(tile[4:5], (4, 128))
    lane32 = iota((32, 128), 1)
    which = iota((32, 128), 0) // 4 % 4
    for k in range(TOP):
        stat = far_s[k]
        m = jnp.sum(jnp.where(lane32 == which, stat, 0.0), axis=1, keepdims=True)
        total = jnp.sum(jnp.where(lane32 == which + PER_KV, stat, 0.0), axis=1, keepdims=True)
        parts.append((far_o[k], m, total))
    summed, _, weight = merged(parts)
    out_ref[...] = (summed / weight).astype(out_ref.dtype)

    others = pl.ds(1, PEERS - 1)
    for buffer, rows, sem in ((msg_out, MSG, msg_send), (res_out, RES, res_send)):
        sent = buffer.at[others, pl.ds(0, rows)]
        pltpu.make_async_copy(sent, sent, sem).wait()


def per_device(queries, request_of, selected, cache_keys, cache_values, recent_keys, recent_values):
    q = queries.reshape(ROWS, KVH * PER_KV, HD).transpose(1, 0, 2).reshape(128, HD)
    blocks = lambda a: a.reshape(PEERS, BLOCK, HD)
    recents = lambda a: a.reshape(ROWS * KVH, RECENT, HD)
    vmem = lambda shape, kind: pltpu.VMEM(shape, kind)
    dma = pltpu.SemaphoreType.DMA
    bf16, f32 = jnp.bfloat16, jnp.float32
    out = pl.pallas_call(
        kernel,
        out_shape=jax.ShapeDtypeStruct((32, HD), bf16),
        in_specs=[pl.BlockSpec(memory_space=pltpu.HBM)] * 7,
        out_specs=pl.BlockSpec(memory_space=pltpu.VMEM),
        scratch_shapes=[
            pltpu.SMEM((ROWS, HEADS, TOP), jnp.int32),
            pltpu.SMEM((ROWS,), jnp.int32),
            vmem((128, HD), bf16),
            vmem((PEERS, BLOCK, HD), bf16),
            vmem((PEERS, BLOCK, HD), bf16),
            vmem((ROWS * KVH, RECENT, HD), bf16),
            vmem((ROWS * KVH, RECENT, HD), bf16),
            vmem((128, HD), bf16),
            vmem((PEERS, 8, HD), bf16),
            vmem((PEERS, 8, HD), bf16),
            vmem((PEERS, 8, HD), f32),
            vmem((PEERS, 8, HD), f32),
            vmem((KVH, 2, 16, HD), f32),
            vmem((NG, HEADS, 2, 16, HD), f32),
            vmem((TOP, 32, HD), f32),
            vmem((TOP, 32, HD), f32),
            dma((7,)),
            dma,
            dma((len(WAVES),)),
            dma,
            dma,
            dma((NG,)),
            dma((NG,)),
        ],
        compiler_params=pltpu.CompilerParams(
            collective_id=0, has_side_effects=True, vmem_limit_bytes=40 * 1024 * 1024
        ),
    )(
        *[
            pltpu.with_memory_space_constraint(a, pltpu.HBM)
            for a in (
                selected, request_of, q, blocks(cache_keys), blocks(cache_values),
                recents(recent_keys), recents(recent_values),
            )
        ]
    )
    return out.reshape(HEADS * PER_KV, ROWS, HD).transpose(1, 0, 2).reshape(ROWS, HEADS * PER_KV * HD)


def solution(mesh):
    return jax.shard_map(
        per_device,
        mesh=mesh,
        in_specs=(
            P("cache", None),
            P("cache"),
            P("cache", "group", None),
            P(None, "group", "cache", None),
            P(None, "group", "cache", None),
            P("cache", None, "group", None),
            P("cache", None, "group", None),
        ),
        out_specs=P("cache", "group"),
        check_vma=False,
    )
```

```python
import functools

import jax
import jax.numpy as jnp
from jax import lax
from jax.experimental import pallas as pl
from jax.experimental.pallas import tpu as pltpu
from jax.sharding import PartitionSpec as P

MESH = pl.DeviceIdType.MESH
NY, NZ, NC, NG = 4, 8, 2, 4
PEERS = NY * NZ * NC
ROWS, HEADS, PER_KV, TOP = 4, 2, 4, 4
KVH, HD, BLOCK = 8, 128, 128
RECENT = 256
SCALE = HD ** (-0.5)
MSG = 6
RES = 5
AHEAD = 2
URGENT = 4
WANTED = ROWS * HEADS * TOP


def signed(j):
    return ((j + 1) // 2) * (2 * (j % 2) - 1)


def hops(chip):
    return abs(signed(chip // NY)) + abs(signed(chip % NY))


CHIPS = sorted(range(NY * NZ), key=hops)
WAVES = [[chip for chip in CHIPS if hops(chip) in at] for at in ((0, 1, 2), (3,), (4,), (5,), (6,))]
WAVE_OF = {chip: n for n, wave in enumerate(WAVES) for chip in wave}


def iota(shape, dim):
    return lax.broadcasted_iota(jnp.int32, shape, dim)


def high_low(p):
    high = p.astype(jnp.bfloat16)
    low = (p - high.astype(jnp.float32)).astype(jnp.bfloat16)
    return jnp.concatenate([high, low], axis=0)


def dot_t(a, b):
    return lax.dot_general(a, b, (((1,), (1,)), ((), ())), preferred_element_type=jnp.float32)


def dot(a, b):
    return jnp.dot(a, b, preferred_element_type=jnp.float32)


def kernel(
    sel_hbm, req_hbm, q_hbm, ck_ref, cv_ref, rk_ref, rv_ref, out_ref,
    sel_ref, req_ref, q_ref, ck, cv, rk, rv, rhs, msg_out, msg_in, res_out, res_in, near_out, near_in, far_o, far_s,
    load_sem, msg_send, msg_recv, res_send, res_recv, near_send, near_recv,
):
    cache = lax.axis_index("cache")
    group = lax.axis_index("group")
    y = lax.div(cache, NZ * NC)
    z = lax.rem(lax.div(cache, NC), NZ)
    c = lax.rem(cache, NC)
    other_z = [lax.rem(z + (NZ + signed(jz)), NZ) * NC for jz in range(NZ)]
    other_y = [lax.rem(y + (NY + signed(jy)), NY) * (NZ * NC) for jy in range(NY)]
    other_c = [c, 1 - c]
    other_yc = [other_y[i // NC] + other_c[i % NC] for i in range(NY * NC)]
    opposite = lambda j, n: 0 if j == 0 else (j + 1 if j % 2 and j + 1 < n else j if j % 2 else j - 1)

    def ahead(j):
        return (other_z[j // 8] + other_yc[j % 8], group)

    def behind(j):
        jz, jy, jc = opposite(j // 8, NZ), opposite(j // NC % NY, NY), j % NC
        return (other_z[jz] + other_yc[jy * NC + jc], group)

    barrier = pltpu.get_barrier_semaphore()
    order = [2 * chip + i for chip in reversed(CHIPS) for i in (1, 0) if chip + i]
    for j in order:
        pl.semaphore_signal(barrier, inc=1, device_id=ahead(j), device_id_type=MESH)
    for dg in range(1, NG):
        pl.semaphore_signal(
            barrier, inc=1, device_id=(cache, lax.rem(group + dg, NG)), device_id_type=MESH
        )

    loads = [
        pltpu.make_async_copy(src, dst, load_sem.at[i])
        for i, (src, dst) in enumerate(
            (
                (sel_hbm, sel_ref), (req_hbm, req_ref), (q_hbm, q_ref),
                (rk_ref, rk), (rv_ref, rv), (ck_ref, ck), (cv_ref, cv),
            )
        )
    ]
    for load in loads:
        load.start()

    loads[0].wait()
    loads[1].wait()

    lane = iota((8, 128), 1)
    wanted_by = [jnp.full((8, 128), -1, jnp.int32) for _ in range(TOP)]
    codes = jnp.zeros((WANTED, 128), jnp.int32)
    code_row = iota((WANTED, 128), 0)
    for r in range(ROWS):
        prompt = req_ref[r]
        for h in range(HEADS):
            here = (lane < 32) & (lane // 16 == h) & (lane % 4 == r)
            for k in range(TOP):
                e = (r * HEADS + h) * TOP + k
                block = sel_ref[r, h, k]
                owner = lax.shift_right_logical(block, 1)
                wanted_by[k] = jnp.where(here, owner, wanted_by[k])
                wanted_by[0] = jnp.where(lane == 32 + e, owner, wanted_by[0])
                code = prompt * 4 + h * 2 + (block - owner * 2) + 1
                codes = jnp.where(code_row == e, code, codes)
    wanted_by = [jnp.broadcast_to(w[0:1], (64, 128)) for w in wanted_by]
    loads[2].wait()
    rhs[0:32, :] = q_ref[pl.ds(pl.multiple_of(group * 32, 32), 32), :]
    rhs[32:64, :] = codes.astype(jnp.float32).astype(jnp.bfloat16)
    rhs[64:128, :] = jnp.zeros((64, 128), jnp.bfloat16)
    table = rhs[...]
    row64 = iota((64, 128), 0)
    lane64 = iota((64, 128), 1)
    half = row64 // 8 % 2
    place = row64 % 8
    col_row = jnp.where(lane64 < 32, lane64 // 4 % 4 + 4 * half, jnp.where(lane64 < 64, 4 - half, 9))
    row_match = place == col_row
    base = jnp.zeros((64, 128), jnp.int32)
    for i in range(8):
        base = jnp.where(row64 // 8 == i, other_yc[i], base)
    for jz in range(NZ):
        owner = base + other_z[jz]
        hit = wanted_by[0] == owner
        for k in range(1, TOP):
            hit = hit | (wanted_by[k] == owner)
        pick = jnp.where(hit & row_match, 1.0, 0.0).astype(jnp.bfloat16)
        msg_out[jz * 8 : (jz + 1) * 8] = dot(pick, table).reshape(8, 8, 128).astype(jnp.bfloat16)

    loads[3].wait()
    loads[4].wait()
    row16 = iota((16, RECENT), 0) % ROWS
    row32 = iota((32, HD), 0) % ROWS
    lane16 = iota((16, HD), 1)

    def recent_scores(h):
        x = q_ref[h * 16 : (h + 1) * 16, :]
        s = dot_t(x, rk[h])
        for r in range(1, ROWS):
            s = jnp.where(row16 == r, dot_t(x, rk[r * KVH + h]), s)
        return s * SCALE

    def recent_rest(h, s):
        m = jnp.max(s, axis=1, keepdims=True)
        p = jnp.exp(s - m)
        total = jnp.sum(p, axis=1, keepdims=True)
        both = high_low(p)
        o = dot(both, rv[h])
        for r in range(1, ROWS):
            o = jnp.where(row32 == r, dot(both, rv[r * KVH + h]), o)
        near_out[h, 0] = o[0:16] + o[16:32]
        near_out[h, 1] = jnp.where(lane16 < 64, m, total)

    pending = []
    for h in range(KVH):
        pending.append((h, recent_scores(h)))
        if h >= AHEAD:
            recent_rest(*pending.pop(0))
    for item in pending:
        recent_rest(*item)

    pl.semaphore_wait(barrier, PEERS - 1 + NG - 1)

    def message(j):
        at = pl.ds(0, MSG) if j % 2 == 0 else pl.ds(8 - MSG, MSG)
        return pltpu.make_async_remote_copy(
            src_ref=msg_out.at[j, at],
            dst_ref=msg_in.at[j, at],
            send_sem=msg_send,
            recv_sem=msg_recv.at[WAVE_OF[j // 2]],
            device_id=ahead(j),
            device_id_type=MESH,
        )

    for j in order[:10] + order[:9:-1]:
        message(j).start()
    own_message = pltpu.make_async_copy(
        msg_out.at[0, pl.ds(0, MSG)], msg_in.at[0, pl.ds(0, MSG)], msg_recv.at[0]
    )
    own_message.start()

    nears = []
    for dg in range(1, NG):
        target = lax.rem(group + dg, NG)
        nears.append(
            pltpu.make_async_remote_copy(
                src_ref=near_out.at[pl.ds(target * HEADS, HEADS)],
                dst_ref=near_in.at[dg],
                send_sem=near_send.at[dg],
                recv_sem=near_recv.at[dg],
                device_id=(cache, target),
                device_id_type=MESH,
            )
        )
    for near in nears:
        near.start()

    loads[5].wait()
    loads[6].wait()

    def result(j):
        return pltpu.make_async_remote_copy(
            src_ref=res_out.at[j, pl.ds(0, RES)],
            dst_ref=res_in.at[cache, pl.ds(0, RES)],
            send_sem=res_send,
            recv_sem=res_recv,
            device_id=behind(j),
            device_id_type=MESH,
        )

    own_result = pltpu.make_async_copy(
        res_out.at[0, pl.ds(0, RES)], res_in.at[cache, pl.ds(0, RES)], res_recv
    )
    row8 = iota((8, 128), 0)
    upper = row8 < PER_KV
    m_first = upper & (lane == row8)
    t_first = upper & (lane == row8 + PER_KV)
    m_second = (~upper) & (lane == row8 - PER_KV)
    t_second = (~upper) & (lane == row8)

    def block_of(x, row):
        code = x[row : row + 1, :].astype(jnp.float32)[0, 0].astype(jnp.int32)
        return jnp.clip(code - 1, 0, PEERS - 1)

    def urgent(jz):
        return other_z[opposite(jz, NZ)] < URGENT * NC

    def send_back(chips):
        for chip in reversed(chips):
            for i in (1, 0):
                if chip + i:
                    result(2 * chip + i).start()
                else:
                    own_result.start()

    def far(n):
        wave = WAVES[n]
        arrived = msg_in.at[pl.ds(0, 2 * len(wave)), pl.ds(0, MSG)]
        pltpu.make_async_copy(arrived, arrived, msg_recv.at[n]).wait()
        pairs = []
        for chip in wave:
            first, second = msg_in[2 * chip], msg_in[2 * chip + 1]
            a, b = block_of(first, 4), block_of(second, 3)
            x = jnp.where(upper, first.astype(jnp.float32), second.astype(jnp.float32))
            pairs.append((x.astype(jnp.bfloat16), a, b))
        scores = []
        for x, a, b in pairs:
            s = dot_t(x, jnp.concatenate([ck[a], ck[b]], axis=0))
            scores.append(jnp.where(upper, s[:, :BLOCK], s[:, BLOCK:]) * SCALE)
        highs = [jnp.max(s, axis=1, keepdims=True) for s in scores]
        weights = [jnp.exp(s - m) for s, m in zip(scores, highs)]
        totals = [jnp.sum(p, axis=1, keepdims=True) for p in weights]
        for chip, (x, a, b), p, m, t in zip(wave, pairs, weights, highs, totals):
            both = high_low(
                jnp.concatenate([jnp.where(upper, p, 0.0), jnp.where(upper, 0.0, p)], axis=1)
            )
            o = dot(both, jnp.concatenate([cv[a], cv[b]], axis=0))
            o = o[0:8] + o[8:16]
            one = jnp.sum(jnp.where(m_first, m, jnp.where(t_first, t, 0.0)), axis=0, keepdims=True)
            two = jnp.sum(jnp.where(m_second, m, jnp.where(t_second, t, 0.0)), axis=0, keepdims=True)
            res_out[2 * chip] = jnp.where(upper, o, one)
            res_out[2 * chip + 1] = jnp.where(upper, pltpu.roll(o, PER_KV, 0), two)
        for jz in range(NZ):
            chips = [chip for chip in wave if chip // NY == jz]
            if chips:
                pl.when(urgent(jz))(lambda: send_back(chips))

    for n in range(len(WAVES)):
        far(n)
    for jz in reversed(range(NZ)):
        chips = [chip for chip in CHIPS if chip // NY == jz]
        pl.when(jnp.logical_not(urgent(jz)))(lambda: send_back(chips))

    for near in nears:
        near.wait()

    def merged(parts):
        peak = functools.reduce(jnp.maximum, [m for _, m, _ in parts])
        summed, weight = 0.0, 0.0
        for o, m, total in parts:
            factor = jnp.exp(m - peak)
            summed = summed + factor * o
            weight = weight + factor * total
        return summed, peak, weight

    parts = []
    for dg in range(NG):
        if dg:
            both = near_in[dg]
        else:
            both = near_out[pl.ds(group * HEADS, HEADS)]
        stat = both[:, 1].reshape(32, 128)
        parts.append((both[:, 0].reshape(32, 128), stat[:, 0:1], stat[:, 64:65]))
    parts = [merged(parts)]

    returned = pl.ds(0, RES)
    pltpu.make_async_copy(res_out.at[:, returned], res_in.at[:, returned], res_recv).wait()

    for r in range(ROWS):
        for h in range(HEADS):
            for k in range(TOP):
                tile = res_in[lax.shift_right_logical(sel_ref[r, h, k], 1)]
                rows = pl.ds(h * 16 + r, 4, stride=4)
                far_o[k, rows, :] = tile[0:4]
                far_s[k, rows, :] = jnp.broadcast_to(tile[4:5], (4, 128))
    lane32 = iota((32, 128), 1)
    which = iota((32, 128), 0) // 4 % 4
    for k in range(TOP):
        stat = far_s[k]
        m = jnp.sum(jnp.where(lane32 == which, stat, 0.0), axis=1, keepdims=True)
        total = jnp.sum(jnp.where(lane32 == which + PER_KV, stat, 0.0), axis=1, keepdims=True)
        parts.append((far_o[k], m, total))
    summed, _, weight = merged(parts)
    out_ref[...] = (summed / weight).astype(out_ref.dtype)

    others = pl.ds(1, PEERS - 1)
    for buffer, rows, sem in ((msg_out, MSG, msg_send), (res_out, RES, res_send)):
        sent = buffer.at[others, pl.ds(0, rows)]
        pltpu.make_async_copy(sent, sent, sem).wait()


def per_device(queries, request_of, selected, cache_keys, cache_values, recent_keys, recent_values):
    q = queries.reshape(ROWS, KVH * PER_KV, HD).transpose(1, 0, 2).reshape(128, HD)
    blocks = lambda a: a.reshape(PEERS, BLOCK, HD)
    recents = lambda a: a.reshape(ROWS * KVH, RECENT, HD)
    vmem = lambda shape, kind: pltpu.VMEM(shape, kind)
    dma = pltpu.SemaphoreType.DMA
    bf16, f32 = jnp.bfloat16, jnp.float32
    out = pl.pallas_call(
        kernel,
        out_shape=jax.ShapeDtypeStruct((32, HD), bf16),
        in_specs=[pl.BlockSpec(memory_space=pltpu.HBM)] * 7,
        out_specs=pl.BlockSpec(memory_space=pltpu.VMEM),
        scratch_shapes=[
            pltpu.SMEM((ROWS, HEADS, TOP), jnp.int32),
            pltpu.SMEM((ROWS,), jnp.int32),
            vmem((128, HD), bf16),
            vmem((PEERS, BLOCK, HD), bf16),
            vmem((PEERS, BLOCK, HD), bf16),
            vmem((ROWS * KVH, RECENT, HD), bf16),
            vmem((ROWS * KVH, RECENT, HD), bf16),
            vmem((128, HD), bf16),
            vmem((PEERS, 8, HD), bf16),
            vmem((PEERS, 8, HD), bf16),
            vmem((PEERS, 8, HD), f32),
            vmem((PEERS, 8, HD), f32),
            vmem((KVH, 2, 16, HD), f32),
            vmem((NG, HEADS, 2, 16, HD), f32),
            vmem((TOP, 32, HD), f32),
            vmem((TOP, 32, HD), f32),
            dma((7,)),
            dma,
            dma((len(WAVES),)),
            dma,
            dma,
            dma((NG,)),
            dma((NG,)),
        ],
        compiler_params=pltpu.CompilerParams(
            collective_id=0, has_side_effects=True, vmem_limit_bytes=40 * 1024 * 1024
        ),
    )(
        *[
            pltpu.with_memory_space_constraint(a, pltpu.HBM)
            for a in (
                selected, request_of, q, blocks(cache_keys), blocks(cache_values),
                recents(recent_keys), recents(recent_values),
            )
        ]
    )
    return out.reshape(HEADS * PER_KV, ROWS, HD).transpose(1, 0, 2).reshape(ROWS, HEADS * PER_KV * HD)


def solution(mesh):
    return jax.shard_map(
        per_device,
        mesh=mesh,
        in_specs=(
            P("cache", None),
            P("cache"),
            P("cache", "group", None),
            P(None, "group", "cache", None),
            P(None, "group", "cache", None),
            P("cache", None, "group", None),
            P("cache", None, "group", None),
        ),
        out_specs=P("cache", "group"),
        check_vma=False,
    )
```
